32 devices in a mesh: groups: 2 (over x), row: 16 (over z, y, core).
Axes of the slice: x: 2, y: 2, z: 4, core: 2. Of those that a mesh axis runs over, the one named last changes fastest.
Arguments:
- tensor: float32 [256, 128, 128], P(('groups', 'row')), parts along dimension 0, may hold values from -6 to 6
- init_second: float32 [256, 512], P('groups'), parts along dimension 0, may hold values from -6 to 6
- init_third: float32 [256, 512], P('groups'), parts along dimension 0, may hold values from -6 to 6
Outputs:
- factor_first: float32 [256, 512], P(('groups', 'row')), parts along dimension 0
- factor_second: float32 [256, 512], P(('groups', 'row')), parts along dimension 0
- factor_third: float32 [256, 512], P('groups'), parts along dimension 0
- weights: float32 [1024], P('groups'), parts along dimension 0
The draws below stay inside these ranges and needn't reach their ends.
There are 2 independent parts, one for each index of `groups`. The reference program is written for one: setup_inputs(seed, part) draws one part's arguments, and reference() takes and returns one part's arrays. A program takes and returns all parts, laid end to end along the dimension named above; each array names one. Nothing has to cross between parts.
All inputs are finite; a program needn't handle non-finite values.
Results may differ from the reference program's by a relative error of at most 0.0001.
Values sent between devices are 32-bit elements; how exact they have to be, the bound alone decides.
A program may use at most 128 MiB of HBM per device.

```python
import math
import jax
import jax.numpy as jnp
from jax import lax

I_DEV = 8
K = 128
R = 512
I = 128
J = 128
N_ROW = 16


def shard_levels(own_key, dims, split, low, largest):
    def one(axis_at, shards_of):
        steps = jax.random.uniform(jax.random.fold_in(jax.random.fold_in(own_key, 6), axis_at), (shards_of,), jnp.float32, low / len(split), largest / len(split))
        return jnp.repeat(jnp.exp(steps), dims[axis_at] // shards_of).reshape((-1,) + (1,) * (len(dims) - axis_at - 1))

    factor_of = one(*split[0])
    for cut in split[1:]:
        factor_of = factor_of * one(*cut)
    return factor_of


def noise(key, shape, width, reach, cuts=(), kind=jnp.bfloat16):
    result = jax.random.normal(key, shape, jnp.float32) * width
    if len(cuts) > 0:
        result = shard_levels(key, shape, cuts, -0.22, 0.18) * result
    return jnp.clip(result, min=-reach, max=reach).astype(kind)


def setup_inputs(seed: int = 0, part: int = 0) -> dict:
    keys = jax.random.split(jax.random.key(seed), 4)
    part_splits = jax.random.split(jax.random.fold_in(keys[3], part), 4)
    tensor = noise(part_splits[0], (I, J, K), 1.0, 6.0, ((0, 16),), jnp.float32)
    init_second = noise(part_splits[1], (J, R), 1.0, 6.0, (), jnp.float32)
    init_third = noise(part_splits[2], (K, R), 1.0, 6.0, (), jnp.float32)
    return {"tensor": tensor, "init_second": init_second, "init_third": init_third}


HIGHEST = lax.Precision.HIGHEST
RIDGE = 0.05
EPSILON = 1e-06

def mean_gram(factor, count):
    return jnp.dot(factor.T.astype(jnp.float32), factor.astype(jnp.float32), precision=HIGHEST, preferred_element_type=jnp.float32) / count

def ridge_solve(right, first, second):
    hadamard = first * second
    shift = RIDGE * jnp.mean(jnp.diagonal(hadamard))
    system = hadamard + shift * jnp.eye(hadamard.shape[0], dtype=jnp.float32)
    lower = jnp.linalg.cholesky(system)
    return jax.scipy.linalg.cho_solve((lower, True), right.T).T

def normalize(raw, gram_raw):
    scales = jnp.sqrt(jnp.diagonal(gram_raw) + EPSILON)
    return (raw / scales, gram_raw / (scales[:, None] * scales[None, :]))

def reference(tensor, init_second, init_third):
    blocks = tensor.reshape(N_ROW, I_DEV, J, K)
    gram_b0 = mean_gram(init_second, J)
    gram_c0 = mean_gram(init_third, K)

    def first_pass(slab_part):
        contracted = jnp.einsum('ijk,kr->ijr', slab_part, init_third, precision=HIGHEST)
        return jnp.einsum('ijr,jr->ir', contracted, init_second, precision=HIGHEST)
    right_a = lax.map(first_pass, blocks).reshape(I, R)
    raw_a = ridge_solve(right_a, gram_b0, gram_c0)
    factor_first, gram_a = normalize(raw_a, mean_gram(raw_a, I))
    rows_a = factor_first.reshape(N_ROW, I_DEV, R)

    def second_pass(running, pair):
        slab_part, factor_rows = pair
        contracted = jnp.einsum('ijk,kr->ijr', slab_part, init_third, precision=HIGHEST)
        return (running + jnp.einsum('ijr,ir->jr', contracted, factor_rows, precision=HIGHEST), None)
    right_b, _ = lax.scan(second_pass, jnp.zeros((J, R), jnp.float32), (blocks, rows_a))
    raw_b = ridge_solve(right_b, gram_a, gram_c0)
    factor_second, gram_b = normalize(raw_b, mean_gram(raw_b, J))

    def third_pass(running, pair):
        slab_part, factor_rows = pair
        product = jnp.einsum('ijk,jr->ikr', slab_part, factor_second, precision=HIGHEST)
        return (running + jnp.einsum('ikr,ir->kr', product, factor_rows, precision=HIGHEST), None)
    right_c, _ = lax.scan(third_pass, jnp.zeros((K, R), jnp.float32), (blocks, rows_a))
    raw_c = ridge_solve(right_c, gram_a, gram_b)
    scale_c = jnp.sqrt(lax.optimization_barrier(jnp.mean(raw_c * raw_c, axis=0)) + EPSILON)
    factor_third = raw_c / scale_c
    weights = scale_c / math.sqrt(I * J)
    return (factor_first, factor_second, factor_third, weights)
```

```python
import functools
import math

import jax
import jax.numpy as jnp
from jax import lax
from jax.experimental import pallas as pl
from jax.experimental.pallas import tpu as pltpu
from jax.sharding import PartitionSpec as P

HIGHEST = lax.Precision.HIGHEST
MESH = pl.DeviceIdType.MESH
RIDGE = 0.05
EPSILON = 1e-06
SOLVE_TOL = 4e-06
MAX_ROUNDS = 2048
UNROLL = 2
VMEM_LIMIT = 56 * 1024 * 1024


def dot(a, b):
    return jnp.dot(a, b, precision=HIGHEST, preferred_element_type=jnp.float32)


def split3(value):
    high = value.astype(jnp.bfloat16).astype(jnp.float32)
    rest = value - high
    middle = rest.astype(jnp.bfloat16).astype(jnp.float32)
    return high, middle, rest - middle


def conjugate_solve(right, first, second, vh_ref, vm_ref, vl_ref):
    size = first.shape[0]
    rows = right.shape[0]
    hadamard = first * second
    eye = lax.broadcasted_iota(jnp.int32, (size, size), 0) == lax.broadcasted_iota(jnp.int32, (size, size), 1)
    diagonal = jnp.sum(jnp.where(eye, hadamard, 0.0), axis=0, keepdims=True)
    mean = jnp.sum(diagonal, axis=1, keepdims=True) / size
    inverse_mean = 1.0 / mean
    system = hadamard * inverse_mean + jnp.where(eye, RIDGE, 0.0)
    high, middle, low = split3(system)
    vh_ref[...] = high.astype(jnp.bfloat16)
    vm_ref[...] = middle.astype(jnp.bfloat16)
    vl_ref[...] = low.astype(jnp.bfloat16)
    precondition = 1.0 / (diagonal * inverse_mean + RIDGE)
    largest = jnp.max(jnp.abs(right), axis=1, keepdims=True)
    largest = jnp.where(largest > 0, largest, 1.0)

    def apply(p):
        ph, pm, plow = split3(p)
        parts = jnp.concatenate([ph, pm, plow], axis=0).astype(jnp.bfloat16)
        by_high = jnp.dot(parts, vh_ref[...], preferred_element_type=jnp.float32)
        by_middle = jnp.dot(parts, vm_ref[...], preferred_element_type=jnp.float32)
        by_low = jnp.dot(parts, vl_ref[...], preferred_element_type=jnp.float32)
        small = by_high[2 * rows :] + by_low[:rows] + by_middle[rows : 2 * rows]
        return by_high[:rows] + (by_high[rows : 2 * rows] + by_middle[:rows] + small)

    def row_sum(value):
        return jnp.sum(value, axis=1, keepdims=True)

    def one(x, r, p, rz):
        q = apply(p)
        curvature = row_sum(p * q)
        alpha = jnp.where(curvature > 0, rz / curvature, 0.0)
        x = x + alpha * p
        r = r - alpha * q
        z = r * precondition
        rz_next = row_sum(r * z)
        beta = jnp.where(rz > 0, rz_next / rz, 0.0)
        return x, r, z + beta * p, rz_next

    def body(carry):
        count, _, x, r, p, rz = carry
        for _ in range(UNROLL):
            x, r, p, rz = one(x, r, p, rz)
        excess = row_sum(r * r) - (SOLVE_TOL * RIDGE) ** 2 * row_sum(x * x)
        return count + 1, jnp.max(excess), x, r, p, rz

    def unfinished(carry):
        return jnp.logical_and(carry[1] > 0, carry[0] < MAX_ROUNDS)

    r = right / largest
    z = r * precondition
    start = (jnp.int32(0), jnp.float32(1.0), jnp.zeros_like(r), r, z, row_sum(r * z))
    x = lax.while_loop(unfinished, body, start)[2]
    return x * (largest * inverse_mean)


def first_kernel(tensor_ref, second_ref, third_ref, raw_ref, contracted_ref, gram_c_ref, vh_ref, vm_ref, vl_ref):
    second = second_ref[...]
    third = third_ref[...]
    rows = []
    for i in range(tensor_ref.shape[0]):
        contracted = dot(tensor_ref[i], third)
        contracted_ref[i] = contracted
        rows.append(jnp.sum(contracted * second, axis=0, keepdims=True))
    right = jnp.concatenate(rows, axis=0)
    gram_c = dot(third.T, third) / third.shape[0]
    gram_c_ref[...] = gram_c
    gram_b = dot(second.T, second) / second.shape[0]
    raw_ref[...] = conjugate_solve(right, gram_b, gram_c, vh_ref, vm_ref, vl_ref)


def solve_kernel(right_ref, first_ref, second_ref, raw_ref, vh_ref, vm_ref, vl_ref):
    raw_ref[...] = conjugate_solve(right_ref[...], first_ref[...], second_ref[...], vh_ref, vm_ref, vl_ref)


def greet(n):
    me = lax.axis_index("row")
    barrier = pltpu.get_barrier_semaphore()
    for step in range(1, n):
        pl.semaphore_signal(barrier, inc=1, device_id={"row": lax.rem(me + step, n)}, device_id_type=MESH)
    return me, lambda: pl.semaphore_wait(barrier, n - 1)


def gather_copies(n, me, src_ref, all_ref, send_sem, recv_sem):
    return [
        pltpu.make_async_remote_copy(
            src_ref=src_ref,
            dst_ref=all_ref.at[me],
            send_sem=send_sem.at[step],
            recv_sem=recv_sem.at[step],
            device_id={"row": lax.rem(me + step, n)},
            device_id_type=MESH,
        )
        for step in range(1, n)
    ]


def scatter_copies(n, me, part_ref, parts_ref, send_sem, recv_sem):
    return [
        pltpu.make_async_remote_copy(
            src_ref=part_ref.at[lax.rem(me + step, n)],
            dst_ref=parts_ref.at[me],
            send_sem=send_sem.at[step],
            recv_sem=recv_sem.at[step],
            device_id={"row": lax.rem(me + step, n)},
            device_id_type=MESH,
        )
        for step in range(1, n)
    ]


def gather_all(n, me, wait_barrier, raw_ref, all_ref, send_sem, recv_sem):
    copies = gather_copies(n, me, raw_ref, all_ref, send_sem, recv_sem)
    wait_barrier()
    for copy in copies:
        copy.start()
    all_ref[me] = raw_ref[...]
    return copies


def scatter_sum(n, me, right, part_ref, parts_ref, send_sem, recv_sem):
    share = right.shape[0] // n
    for device in range(n):
        part_ref[device] = right[device * share : (device + 1) * share]
    copies = scatter_copies(n, me, part_ref, parts_ref, send_sem, recv_sem)
    for copy in copies:
        copy.start()
    parts_ref[me] = part_ref[me]
    return copies


def unit_columns(all_raw):
    raw = all_raw.reshape(-1, all_raw.shape[-1])
    scales = jnp.sqrt(jnp.sum(raw * raw, axis=0, keepdims=True) / raw.shape[0] + EPSILON)
    return raw, scales


def first_exchange(
    n, raw_ref, contracted_ref, factor_ref, gram_ref, right_ref, all_ref, part_ref, parts_ref, gs, gr, ss, sr
):
    me, wait_barrier = greet(n)
    gathers = gather_all(n, me, wait_barrier, raw_ref, all_ref, gs, gr)
    for copy in gathers:
        copy.wait()
    raw, scales = unit_columns(all_ref[...])
    own = raw_ref[...] / scales
    factor_ref[...] = own
    right = contracted_ref[0] * own[0:1]
    for i in range(1, own.shape[0]):
        right = right + contracted_ref[i] * own[i : i + 1]
    scatters = scatter_sum(n, me, right, part_ref, parts_ref, ss, sr)
    factor = raw / scales
    gram_ref[...] = dot(factor.T, factor) / factor.shape[0]
    for copy in scatters:
        copy.wait()
    right_ref[...] = jnp.sum(parts_ref[...], axis=0)


def second_exchange(
    n, raw_ref, tensor_ref, first_ref, factor_ref, gram_ref, right_ref, all_ref, part_ref, parts_ref, gs, gr, ss, sr
):
    me, wait_barrier = greet(n)
    local_rows, second_cells, depth_cells = tensor_ref.shape
    turned = tensor_ref[...].reshape(local_rows * second_cells, depth_cells).T
    gathers = gather_all(n, me, wait_barrier, raw_ref, all_ref, gs, gr)
    for copy in gathers:
        copy.wait()
    raw, scales = unit_columns(all_ref[...])
    factor = raw / scales
    factor_ref[...] = raw_ref[...] / scales
    first = first_ref[...]
    pairs = jnp.concatenate([factor * first[i : i + 1] for i in range(local_rows)], axis=0)
    right = dot(turned, pairs)
    scatters = scatter_sum(n, me, right, part_ref, parts_ref, ss, sr)
    gram_ref[...] = dot(factor.T, factor) / factor.shape[0]
    for copy in scatters:
        copy.wait()
    right_ref[...] = jnp.sum(parts_ref[...], axis=0)


def third_exchange(n, total, raw_ref, factor_ref, weights_ref, all_ref, gs, gr):
    me, wait_barrier = greet(n)
    gathers = gather_all(n, me, wait_barrier, raw_ref, all_ref, gs, gr)
    for copy in gathers:
        copy.wait()
    raw = all_ref[...]
    square = jnp.sum(jnp.sum(raw * raw, axis=0), axis=0, keepdims=True)
    scales = jnp.sqrt(square / (raw.shape[0] * raw.shape[1]) + EPSILON)
    factor_ref[...] = raw / scales[None]
    weights_ref[...] = scales / math.sqrt(total)


def f32(*shape):
    return jax.ShapeDtypeStruct(shape, jnp.float32)


def call(kernel, name, out_shape, scratch, collective_id=None):
    vmem = pl.BlockSpec(memory_space=pltpu.VMEM)
    params = {} if collective_id is None else {"collective_id": collective_id, "has_side_effects": True}
    return pl.pallas_call(
        kernel,
        name=name,
        out_shape=out_shape,
        out_specs=jax.tree.map(lambda _: vmem, out_shape),
        scratch_shapes=scratch,
        compiler_params=pltpu.CompilerParams(vmem_limit_bytes=VMEM_LIMIT, **params),
    )


def on_device(tensor, init_second, init_third):
    local_rows, second_cells, depth_cells = tensor.shape
    rank = init_second.shape[1]
    n = lax.axis_size("row")
    total_first = local_rows * n
    second_own, depth_own = second_cells // n, depth_cells // n
    split = [pltpu.VMEM((rank, rank), jnp.bfloat16)] * 3
    sems = [pltpu.SemaphoreType.DMA((n,))] * 2

    def buffers(rows, shares):
        return [pltpu.VMEM((n, rows, rank), jnp.float32)] + [pltpu.VMEM((n, shares, rank), jnp.float32)] * 2

    def solve(right, first, second):
        rows = right.shape[0]
        padded = -(-rows // 8) * 8
        if padded != rows:
            right = jnp.pad(right, ((0, padded - rows), (0, 0)))
        raw = call(solve_kernel, "solve", f32(padded, rank), split)(right, first, second)
        return raw[:rows]

    raw_a, contracted, gram_c0 = call(
        first_kernel,
        "first",
        (f32(local_rows, rank), f32(local_rows, second_cells, rank), f32(rank, rank)),
        split,
    )(tensor, init_second, init_third)
    factor_first, gram_a, right_b = call(
        functools.partial(first_exchange, n),
        "first_exchange",
        (f32(local_rows, rank), f32(rank, rank), f32(second_own, rank)),
        buffers(local_rows, second_own) + sems * 2,
        0,
    )(raw_a, contracted)
    raw_b = solve(right_b, gram_a, gram_c0)
    factor_second, gram_b, right_c = call(
        functools.partial(second_exchange, n),
        "second_exchange",
        (f32(second_own, rank), f32(rank, rank), f32(depth_own, rank)),
        buffers(second_own, depth_own) + sems * 2,
        1,
    )(raw_b, tensor, factor_first)
    raw_c = solve(right_c, gram_a, gram_b)
    factor_third, weights = call(
        functools.partial(third_exchange, n, total_first * second_cells),
        "third_exchange",
        (f32(n, depth_own, rank), f32(1, rank)),
        [pltpu.VMEM((n, depth_own, rank), jnp.float32)] + sems,
        2,
    )(raw_c)
    return (factor_first, factor_second, factor_third.reshape(depth_cells, rank), weights.reshape(rank))


def solution(mesh):
    in_specs = (P(("groups", "row"), None, None), P("groups", None), P("groups", None))
    out_specs = (
        P(("groups", "row"), None),
        P(("groups", "row"), None),
        P("groups", None),
        P("groups"),
    )
    return jax.shard_map(
        on_device, mesh=mesh, in_specs=in_specs, out_specs=out_specs, check_vma=False
    )
```

```python
import functools
import math

import jax
import jax.numpy as jnp
from jax import lax
from jax.experimental import pallas as pl
from jax.experimental.pallas import tpu as pltpu
from jax.sharding import PartitionSpec as P

HIGHEST = lax.Precision.HIGHEST
MESH = pl.DeviceIdType.MESH
RIDGE = 0.05
EPSILON = 1e-06
SOLVE_TOL = 4e-06
MAX_ROUNDS = 2048
UNROLL = 3
VMEM_LIMIT = 32 * 1024 * 1024


def dot(a, b):
    return jnp.dot(a, b, precision=HIGHEST, preferred_element_type=jnp.float32)


def split3(value):
    high = value.astype(jnp.bfloat16).astype(jnp.float32)
    rest = value - high
    middle = rest.astype(jnp.bfloat16).astype(jnp.float32)
    return high, middle, rest - middle


def prepare(first, second, vh_ref, vm_ref, vl_ref):
    size = first.shape[0]
    hadamard = first * second
    eye = lax.broadcasted_iota(jnp.int32, (size, size), 0) == lax.broadcasted_iota(jnp.int32, (size, size), 1)
    diagonal = jnp.sum(jnp.where(eye, hadamard, 0.0), axis=0, keepdims=True)
    mean = jnp.sum(diagonal, axis=1, keepdims=True) / size
    inverse_mean = 1.0 / mean
    system = hadamard * inverse_mean + jnp.where(eye, RIDGE, 0.0)
    high, middle, low = split3(system)
    vh_ref[...] = high.astype(jnp.bfloat16)
    vm_ref[...] = middle.astype(jnp.bfloat16)
    vl_ref[...] = low.astype(jnp.bfloat16)
    return 1.0 / (diagonal * inverse_mean + RIDGE), jnp.broadcast_to(inverse_mean, diagonal.shape)


def conjugate_solve(right, precondition, inverse_mean, vh_ref, vm_ref, vl_ref):
    rows = right.shape[0]
    largest = jnp.max(jnp.abs(right), axis=1, keepdims=True)
    largest = jnp.where(largest > 0, largest, 1.0)

    def apply(p):
        ph, pm, plow = split3(p)
        parts = jnp.concatenate([ph, pm, plow], axis=0).astype(jnp.bfloat16)
        by_high = jnp.dot(parts, vh_ref[...], preferred_element_type=jnp.float32)
        by_middle = jnp.dot(parts, vm_ref[...], preferred_element_type=jnp.float32)
        by_low = jnp.dot(parts, vl_ref[...], preferred_element_type=jnp.float32)
        small = by_high[2 * rows :] + by_low[:rows] + by_middle[rows : 2 * rows]
        return by_high[:rows] + (by_high[rows : 2 * rows] + by_middle[:rows] + small)

    def row_sum(value):
        return jnp.sum(value, axis=1, keepdims=True)

    def one(x, r, p, rz):
        q = apply(p)
        curvature = row_sum(p * q)
        alpha = jnp.where(curvature > 0, rz / curvature, 0.0)
        x = x + alpha * p
        r = r - alpha * q
        z = r * precondition
        rz_next = row_sum(r * z)
        beta = jnp.where(rz > 0, rz_next / rz, 0.0)
        return x, r, z + beta * p, rz_next

    def body(carry):
        count, _, x, r, p, rz = carry
        for _ in range(UNROLL):
            x, r, p, rz = one(x, r, p, rz)
        excess = row_sum(r * r) - (SOLVE_TOL * RIDGE) ** 2 * row_sum(x * x)
        return count + 1, jnp.max(excess), x, r, p, rz

    def unfinished(carry):
        return jnp.logical_and(carry[1] > 0, carry[0] < MAX_ROUNDS)

    r = right / largest
    z = r * precondition
    start = (jnp.int32(0), jnp.float32(1.0), jnp.zeros_like(r), r, z, row_sum(r * z))
    x = lax.while_loop(unfinished, body, start)[2]
    return x * (largest * inverse_mean)


def gram(factor):
    return dot(factor.T, factor) / factor.shape[0]


def first_kernel(tensor_ref, second_ref, third_ref, raw_ref, gram_c_ref, vh_ref, vm_ref, vl_ref):
    second = second_ref[...]
    third = third_ref[...]
    gram_c = gram(third)
    gram_c_ref[...] = gram_c
    scales = prepare(gram(second), gram_c, vh_ref, vm_ref, vl_ref)
    rows = []
    for i in range(tensor_ref.shape[0]):
        rows.append(jnp.sum(dot(tensor_ref[i], third) * second, axis=0, keepdims=True))
    raw_ref[...] = conjugate_solve(jnp.concatenate(rows, axis=0), *scales, vh_ref, vm_ref, vl_ref)


def solve_kernel(right_ref, scales_ref, vh_ref, vm_ref, vl_ref, factor_ref, raw_ref, out_ref):
    out_ref[...] = factor_ref[...]
    raw_ref[...] = conjugate_solve(right_ref[...], scales_ref[0:1], scales_ref[1:2], vh_ref, vm_ref, vl_ref)


def last_kernel(total, raw_ref, factor_ref, weights_ref):
    raw = raw_ref[...]
    square = jnp.sum(jnp.sum(raw * raw, axis=0), axis=0, keepdims=True)
    scales = jnp.sqrt(square / (raw.shape[0] * raw.shape[1]) + EPSILON)
    factor_ref[...] = raw / scales[None]
    weights_ref[...] = scales / math.sqrt(total)


class Place:
    def __init__(self, n):
        self.n = n
        self.chips = n // 2
        self.me = lax.axis_index("row")
        self.chip = self.me // 2
        self.core = lax.rem(self.me, 2)
        self.partner = self.chip * 2 + 1 - self.core

    def chip_after(self, step):
        return lax.rem(self.chip + step, self.chips)

    def chip_before(self, step):
        return lax.rem(self.chip + self.chips - step, self.chips)

    def greet(self):
        barrier = pltpu.get_barrier_semaphore()
        for step in range(1, self.n):
            device = {"row": lax.rem(self.me + step, self.n)}
            pl.semaphore_signal(barrier, inc=1, device_id=device, device_id_type=MESH)
        return barrier

    def send(self, src, dst, sems, at, device):
        return pltpu.make_async_remote_copy(
            src_ref=src,
            dst_ref=dst,
            send_sem=sems.at[0, at],
            recv_sem=sems.at[1, at],
            device_id={"row": device},
            device_id_type=MESH,
        )


def gather_start(place, raw_ref, all_ref, sems):
    own = all_ref.at[place.me]
    copies = []
    for step in range(1, place.chips):
        device = place.chip_after(step) * 2 + place.core
        copies.append(place.send(raw_ref, own, sems, step, device))
    copies.append(place.send(raw_ref, own, sems, 0, place.partner))
    for copy in copies:
        copy.start()
    all_ref[place.me] = raw_ref[...]
    return copies


def gather_finish(place, copies, all_ref, sems):
    forwards = []
    for step in range(1, place.chips):
        copies[step - 1].wait_recv()
        slot = all_ref.at[place.chip_before(step) * 2 + place.core]
        forward = place.send(slot, slot, sems, step, place.partner)
        forward.start()
        forwards.append(forward)
    copies[-1].wait_recv()
    for forward in forwards:
        forward.wait_recv()
    return copies + forwards


def split_parts(place, right, part_ref):
    share = right.shape[0] // place.n
    for device in range(place.n):
        part_ref[device % 2, device // 2] = right[device * share : (device + 1) * share]


def pair_start(place, part_ref, pair_ref, sems):
    copy = place.send(part_ref.at[1 - place.core], pair_ref, sems, 0, place.partner)
    copy.start()
    return copy


def scatter_start(place, pair_copy, part_ref, pair_ref, parts_ref, sems):
    pair_copy.wait()
    part_ref[place.core] = part_ref[place.core] + pair_ref[...]
    copies = []
    for step in range(1, place.chips):
        chip = place.chip_after(step)
        copy = place.send(
            part_ref.at[place.core, chip], parts_ref.at[place.chip], sems, step, chip * 2 + place.core
        )
        copy.start()
        copies.append(copy)
    parts_ref[place.chip] = part_ref[place.core, place.chip]
    return copies


def scatter_finish(copies, parts_ref):
    for copy in copies:
        copy.wait_recv()
    return jnp.sum(parts_ref[...], axis=0)


def unit_columns(all_raw):
    raw = all_raw.reshape(-1, all_raw.shape[-1])
    scales = jnp.sqrt(jnp.sum(raw * raw, axis=0, keepdims=True) / raw.shape[0] + EPSILON)
    return raw / scales, scales


def first_exchange(
    n, raw_ref, tensor_ref, third_ref, gram_c_ref, factor_ref, gram_ref, right_ref, scales_ref, vh_ref, vm_ref, vl_ref,
    all_ref, part_ref, pair_ref, parts_ref, gather_sems, forward_sems, scatter_sems
):
    place = Place(n)
    barrier = place.greet()
    raw = raw_ref[...]
    local_rows = tensor_ref.shape[0]
    slabs = jnp.concatenate([tensor_ref[i] for i in range(local_rows)], axis=1)
    third = third_ref[...]
    pairs = jnp.concatenate([third * raw[i : i + 1] for i in range(local_rows)], axis=0)
    split_parts(place, dot(slabs, pairs), part_ref)
    pl.semaphore_wait(barrier, n - 1)
    pair_copy = pair_start(place, part_ref, pair_ref, scatter_sems)
    gathers = gather_start(place, raw_ref, all_ref, gather_sems)
    scatters = scatter_start(place, pair_copy, part_ref, pair_ref, parts_ref, scatter_sems)
    gathers = gather_finish(place, gathers, all_ref, forward_sems)
    factor, scales = unit_columns(all_ref[...])
    factor_ref[...] = raw / scales
    gram_a = gram(factor)
    gram_ref[...] = gram_a
    scales_ref[0:1], scales_ref[1:2] = prepare(gram_a, gram_c_ref[...], vh_ref, vm_ref, vl_ref)
    right_ref[...] = scatter_finish(scatters, parts_ref) / scales
    for copy in gathers + scatters:
        copy.wait_send()


def second_exchange(
    n, raw_ref, tensor_ref, first_ref, gram_a_ref, factor_ref, right_ref, scales_ref, vh_ref, vm_ref, vl_ref,
    all_ref, part_ref, pair_ref, parts_ref, gather_sems, forward_sems, scatter_sems
):
    place = Place(n)
    barrier = place.greet()
    local_rows, second_cells, depth_cells = tensor_ref.shape
    turned = tensor_ref[...].reshape(local_rows * second_cells, depth_cells).T
    pl.semaphore_wait(barrier, n - 1)
    gathers = gather_start(place, raw_ref, all_ref, gather_sems)
    gathers = gather_finish(place, gathers, all_ref, forward_sems)
    factor, scales = unit_columns(all_ref[...])
    factor_ref[...] = raw_ref[...] / scales
    first = first_ref[...]
    pairs = jnp.concatenate([factor * first[i : i + 1] for i in range(local_rows)], axis=0)
    split_parts(place, dot(turned, pairs), part_ref)
    pair_copy = pair_start(place, part_ref, pair_ref, scatter_sems)
    gram_b = gram(factor)
    scatters = scatter_start(place, pair_copy, part_ref, pair_ref, parts_ref, scatter_sems)
    scales_ref[0:1], scales_ref[1:2] = prepare(gram_a_ref[...], gram_b, vh_ref, vm_ref, vl_ref)
    right_ref[...] = scatter_finish(scatters, parts_ref)
    for copy in gathers + scatters:
        copy.wait_send()


def third_exchange(n, raw_ref, all_out_ref, all_ref, gather_sems, forward_sems):
    place = Place(n)
    barrier = place.greet()
    pl.semaphore_wait(barrier, n - 1)
    gathers = gather_start(place, raw_ref, all_ref, gather_sems)
    gathers = gather_finish(place, gathers, all_ref, forward_sems)
    all_out_ref[...] = all_ref[...]
    for copy in gathers:
        copy.wait_send()


def f32(*shape):
    return jax.ShapeDtypeStruct(shape, jnp.float32)


def call(kernel, name, out_shape, scratch, collective_id=None):
    vmem = pl.BlockSpec(memory_space=pltpu.VMEM)
    params = {} if collective_id is None else {"collective_id": collective_id, "has_side_effects": True}
    return pl.pallas_call(
        kernel,
        name=name,
        out_shape=out_shape,
        out_specs=jax.tree.map(lambda _: vmem, out_shape),
        scratch_shapes=scratch,
        compiler_params=pltpu.CompilerParams(vmem_limit_bytes=VMEM_LIMIT, **params),
    )


def on_device(tensor, init_second, init_third):
    local_rows, second_cells, depth_cells = tensor.shape
    rank = init_second.shape[1]
    n = lax.axis_size("row")
    chips = n // 2
    second_own, depth_own = second_cells // n, depth_cells // n
    system = [jax.ShapeDtypeStruct((rank, rank), jnp.bfloat16)] * 3
    split = [pltpu.VMEM((rank, rank), jnp.bfloat16)] * 3
    gather_sems = pltpu.SemaphoreType.DMA((2, chips))

    def buffers(rows, share):
        return [
            pltpu.VMEM((n, rows, rank), jnp.float32),
            pltpu.VMEM((2, chips, share, rank), jnp.float32),
            pltpu.VMEM((chips, share, rank), jnp.float32),
            pltpu.VMEM((chips, share, rank), jnp.float32),
            gather_sems,
            gather_sems,
            gather_sems,
        ]

    def solve(right, scales, parts, factor):
        rows = right.shape[0]
        padded = -(-rows // 8) * 8
        if padded != rows:
            right = jnp.pad(right, ((0, padded - rows), (0, 0)))
        raw, out = call(solve_kernel, "solve", (f32(padded, rank), f32(*factor.shape)), [])(
            right, scales, *parts, factor
        )
        return raw[:rows], out

    raw_a, gram_c0 = call(first_kernel, "first", (f32(local_rows, rank), f32(rank, rank)), split)(
        tensor, init_second, init_third
    )
    factor_first, gram_a, right_b, scales_b, *parts_b = call(
        functools.partial(first_exchange, n),
        "first_exchange",
        (f32(local_rows, rank), f32(rank, rank), f32(second_own, rank), f32(2, rank), *system),
        buffers(local_rows, second_own),
        0,
    )(raw_a, tensor, init_third, gram_c0)
    raw_b, factor_first_out = solve(right_b, scales_b, parts_b, factor_first)
    factor_second, right_c, scales_c, *parts_c = call(
        functools.partial(second_exchange, n),
        "second_exchange",
        (f32(second_own, rank), f32(depth_own, rank), f32(2, rank), *system),
        buffers(second_own, depth_own),
        1,
    )(raw_b, tensor, factor_first, gram_a)
    raw_c, factor_second_out = solve(right_c, scales_c, parts_c, factor_second)
    all_c = call(
        functools.partial(third_exchange, n),
        "third_exchange",
        f32(n, depth_own, rank),
        [pltpu.VMEM((n, depth_own, rank), jnp.float32), gather_sems, gather_sems],
        2,
    )(raw_c)
    factor_third, weights = call(
        functools.partial(last_kernel, local_rows * n * second_cells),
        "last",
        (f32(n, depth_own, rank), f32(1, rank)),
        [],
    )(all_c)
    return (
        factor_first_out,
        factor_second_out,
        factor_third.reshape(depth_cells, rank),
        weights.reshape(rank),
    )


def solution(mesh):
    in_specs = (P(("groups", "row"), None, None), P("groups", None), P("groups", None))
    out_specs = (
        P(("groups", "row"), None),
        P(("groups", "row"), None),
        P("groups", None),
        P("groups"),
    )
    return jax.shard_map(
        on_device, mesh=mesh, in_specs=in_specs, out_specs=out_specs, check_vma=False
    )
```

```python
import functools
import math

import jax
import jax.numpy as jnp
from jax import lax
from jax.experimental import pallas as pl
from jax.experimental.pallas import tpu as pltpu
from jax.sharding import PartitionSpec as P

HIGHEST = lax.Precision.HIGHEST
MESH = pl.DeviceIdType.MESH
RIDGE = 0.05
EPSILON = 1e-06
SOLVE_TOL = 4e-06
MAX_ROUNDS = 2048
UNROLL = 3
VMEM_LIMIT = 40 * 1024 * 1024
FIRST_LIMIT = 63 * 1024 * 1024


def dot(a, b):
    return jnp.dot(a, b, precision=HIGHEST, preferred_element_type=jnp.float32)


def split3(value):
    high = value.astype(jnp.bfloat16).astype(jnp.float32)
    rest = value - high
    middle = rest.astype(jnp.bfloat16).astype(jnp.float32)
    return high, middle, rest - middle


def prepare(first, second, vh_ref, vm_ref, vl_ref):
    size = first.shape[0]
    hadamard = first * second
    eye = lax.broadcasted_iota(jnp.int32, (size, size), 0) == lax.broadcasted_iota(jnp.int32, (size, size), 1)
    diagonal = jnp.sum(jnp.where(eye, hadamard, 0.0), axis=0, keepdims=True)
    mean = jnp.sum(diagonal, axis=1, keepdims=True) / size
    inverse_mean = 1.0 / mean
    system = hadamard * inverse_mean + jnp.where(eye, RIDGE, 0.0)
    high, middle, low = split3(system)
    vh_ref[...] = high.astype(jnp.bfloat16)
    vm_ref[...] = middle.astype(jnp.bfloat16)
    vl_ref[...] = low.astype(jnp.bfloat16)
    return 1.0 / (diagonal * inverse_mean + RIDGE), jnp.broadcast_to(inverse_mean, diagonal.shape)


def conjugate_solve(right, precondition, inverse_mean, vh_ref, vm_ref, vl_ref):
    rows = right.shape[0]
    largest = jnp.max(jnp.abs(right), axis=1, keepdims=True)
    largest = jnp.where(largest > 0, largest, 1.0)

    def apply(p):
        ph, pm, plow = split3(p)
        parts = jnp.concatenate([ph, pm, plow], axis=0).astype(jnp.bfloat16)
        by_high = jnp.dot(parts, vh_ref[...], preferred_element_type=jnp.float32)
        by_middle = jnp.dot(parts, vm_ref[...], preferred_element_type=jnp.float32)
        by_low = jnp.dot(parts, vl_ref[...], preferred_element_type=jnp.float32)
        small = by_high[2 * rows :] + by_low[:rows] + by_middle[rows : 2 * rows]
        return by_high[:rows] + (by_high[rows : 2 * rows] + by_middle[:rows] + small)

    def row_sum(value):
        return jnp.sum(value, axis=1, keepdims=True)

    def one(x, r, p, rz):
        q = apply(p)
        curvature = row_sum(p * q)
        alpha = jnp.where(curvature > 0, rz / curvature, 0.0)
        x = x + alpha * p
        r = r - alpha * q
        z = r * precondition
        rz_next = row_sum(r * z)
        beta = jnp.where(rz > 0, rz_next / rz, 0.0)
        return x, r, z + beta * p, rz_next

    def body(carry):
        count, _, x, r, p, rz = carry
        for _ in range(UNROLL):
            x, r, p, rz = one(x, r, p, rz)
        excess = row_sum(r * r) - (SOLVE_TOL * RIDGE) ** 2 * row_sum(x * x)
        return count + 1, jnp.max(excess), x, r, p, rz

    def unfinished(carry):
        return jnp.logical_and(carry[1] > 0, carry[0] < MAX_ROUNDS)

    r = right / largest
    z = r * precondition
    start = (jnp.int32(0), jnp.float32(1.0), jnp.zeros_like(r), r, z, row_sum(r * z))
    x = lax.while_loop(unfinished, body, start)[2]
    return x * (largest * inverse_mean)


def gram(factor):
    return dot(factor.T, factor) / factor.shape[0]


def first_kernel(
    tensor_hbm, second_hbm, third_hbm, raw_ref, vh_ref, vm_ref, vl_ref, tensor_ref, second_ref, third_ref, sems
):
    loads = [
        pltpu.make_async_copy(source, target, sems.at[at])
        for at, (source, target) in enumerate(
            ((third_hbm, third_ref), (second_hbm, second_ref), (tensor_hbm, tensor_ref))
        )
    ]
    for load in loads:
        load.start()
    loads[0].wait()
    third = third_ref[...]
    gram_c = gram(third)
    loads[1].wait()
    second = second_ref[...]
    scales = prepare(gram(second), gram_c, vh_ref, vm_ref, vl_ref)
    loads[2].wait()
    rows = []
    for i in range(tensor_ref.shape[0]):
        rows.append(jnp.sum(dot(tensor_ref[i], third) * second, axis=0, keepdims=True))
    raw_ref[...] = conjugate_solve(jnp.concatenate(rows, axis=0), *scales, vh_ref, vm_ref, vl_ref)


def solve_kernel(right_ref, scales_ref, vh_ref, vm_ref, vl_ref, factor_ref, raw_ref, out_ref):
    out_ref[...] = factor_ref[...]
    raw_ref[...] = conjugate_solve(right_ref[...], scales_ref[0:1], scales_ref[1:2], vh_ref, vm_ref, vl_ref)


def last_kernel(total, raw_ref, factor_ref, weights_ref):
    raw = raw_ref[...]
    square = jnp.sum(jnp.sum(raw * raw, axis=0), axis=0, keepdims=True)
    scales = jnp.sqrt(square / (raw.shape[0] * raw.shape[1]) + EPSILON)
    factor_ref[...] = raw / scales[None]
    weights_ref[...] = scales / math.sqrt(total)


class Place:
    def __init__(self, n):
        self.n = n
        self.chips = n // 2
        self.me = lax.axis_index("row")
        self.chip = self.me // 2
        self.core = lax.rem(self.me, 2)
        self.partner = self.chip * 2 + 1 - self.core

    def chip_after(self, step):
        return lax.rem(self.chip + step, self.chips)

    def chip_before(self, step):
        return lax.rem(self.chip + self.chips - step, self.chips)

    def greet(self):
        barrier = pltpu.get_barrier_semaphore()
        for step in range(1, self.chips):
            device = {"row": self.chip_after(step) * 2 + self.core}
            pl.semaphore_signal(barrier, inc=1, device_id=device, device_id_type=MESH)
        pl.semaphore_signal(barrier, inc=1, device_id={"row": self.partner}, device_id_type=MESH)
        return lambda: pl.semaphore_wait(barrier, self.chips)

    def send(self, src, dst, sems, at, device):
        return pltpu.make_async_remote_copy(
            src_ref=src,
            dst_ref=dst,
            send_sem=sems.at[0, at],
            recv_sem=sems.at[1, at],
            device_id={"row": device},
            device_id_type=MESH,
        )


def gather_start(place, raw_ref, all_ref, sems):
    own = all_ref.at[place.me]
    copies = []
    for step in range(1, place.chips):
        device = place.chip_after(step) * 2 + place.core
        copies.append(place.send(raw_ref, own, sems, step, device))
    copies.append(place.send(raw_ref, own, sems, 0, place.partner))
    for copy in copies:
        copy.start()
    all_ref[place.me] = raw_ref[...]
    return copies


def gather_finish(place, copies, all_ref, sems):
    forwards = []
    for step in range(1, place.chips):
        copies[step - 1].wait_recv()
        slot = all_ref.at[place.chip_before(step) * 2 + place.core]
        forward = place.send(slot, slot, sems, step, place.partner)
        forward.start()
        forwards.append(forward)
    copies[-1].wait_recv()
    for forward in forwards:
        forward.wait_recv()
    return copies + forwards


def split_parts(place, right, part_ref):
    share = right.shape[0] // place.n
    for device in range(place.n):
        part_ref[device % 2, device // 2] = right[device * share : (device + 1) * share]


def pair_start(place, part_ref, pair_ref, sems):
    copy = place.send(part_ref.at[1 - place.core], pair_ref, sems, 0, place.partner)
    copy.start()
    return copy


def scatter_start(place, pair_copy, part_ref, pair_ref, parts_ref, sems):
    pair_copy.wait()
    part_ref[place.core] = part_ref[place.core] + pair_ref[...]
    copies = []
    for step in range(1, place.chips):
        chip = place.chip_after(step)
        copy = place.send(
            part_ref.at[place.core, chip], parts_ref.at[place.chip], sems, step, chip * 2 + place.core
        )
        copy.start()
        copies.append(copy)
    parts_ref[place.chip] = part_ref[place.core, place.chip]
    return copies


def scatter_finish(copies, parts_ref):
    for copy in copies:
        copy.wait_recv()
    return jnp.sum(parts_ref[...], axis=0)


def unit_columns(all_raw):
    raw = all_raw.reshape(-1, all_raw.shape[-1])
    scales = jnp.sqrt(jnp.sum(raw * raw, axis=0, keepdims=True) / raw.shape[0] + EPSILON)
    return raw / scales, scales


def exchange(place, wait_barrier, terms, other_gram, raw_ref, right_ref, scales_ref, vh_ref, vm_ref, vl_ref,
             all_ref, part_ref, pair_ref, parts_ref, gather_sems, forward_sems, scatter_sems):
    split_parts(place, terms, part_ref)
    wait_barrier()
    pair_copy = pair_start(place, part_ref, pair_ref, scatter_sems)
    gathers = gather_start(place, raw_ref, all_ref, gather_sems)
    scatters = scatter_start(place, pair_copy, part_ref, pair_ref, parts_ref, scatter_sems)
    gathers = gather_finish(place, gathers, all_ref, forward_sems)
    factor, scales = unit_columns(all_ref[...])
    own_gram = gram(factor)
    scales_ref[0:1], scales_ref[1:2] = prepare(own_gram, other_gram, vh_ref, vm_ref, vl_ref)
    right_ref[...] = scatter_finish(scatters, parts_ref) / scales
    for copy in gathers + scatters:
        copy.wait_send()
    return factor, own_gram, scales


def first_exchange(n, raw_ref, tensor_ref, third_ref, factor_ref, all_factor_ref, gram_ref, *refs):
    place = Place(n)
    wait_barrier = place.greet()
    raw = raw_ref[...]
    local_rows = tensor_ref.shape[0]
    slabs = jnp.concatenate([tensor_ref[i] for i in range(local_rows)], axis=1)
    third = third_ref[...]
    pairs = jnp.concatenate([third * raw[i : i + 1] for i in range(local_rows)], axis=0)
    terms = dot(slabs, pairs)
    factor, gram_a, scales = exchange(place, wait_barrier, terms, gram(third), raw_ref, *refs)
    all_factor_ref[...] = factor
    gram_ref[...] = gram_a
    factor_ref[...] = raw / scales


def second_exchange(n, raw_ref, swapped_ref, first_ref, gram_a_ref, factor_ref, *refs):
    place = Place(n)
    wait_barrier = place.greet()
    raw = raw_ref[...]
    turned = swapped_ref[...].reshape(-1, swapped_ref.shape[-1]).T
    first = first_ref[...]
    pairs = jnp.concatenate([raw * first[i : i + 1] for i in range(first.shape[0])], axis=0)
    terms = dot(turned, pairs)
    _, _, scales = exchange(place, wait_barrier, terms, gram_a_ref[...], raw_ref, *refs)
    factor_ref[...] = raw / scales


def third_exchange(n, raw_ref, all_out_ref, all_ref, gather_sems, forward_sems):
    place = Place(n)
    wait_barrier = place.greet()
    wait_barrier()
    gathers = gather_start(place, raw_ref, all_ref, gather_sems)
    gathers = gather_finish(place, gathers, all_ref, forward_sems)
    all_out_ref[...] = all_ref[...]
    for copy in gathers:
        copy.wait_send()


def f32(*shape):
    return jax.ShapeDtypeStruct(shape, jnp.float32)


def call(kernel, name, out_shape, scratch, collective_id=None, in_specs=None, limit=VMEM_LIMIT):
    vmem = pl.BlockSpec(memory_space=pltpu.VMEM)
    params = {} if collective_id is None else {"collective_id": collective_id, "has_side_effects": True}
    return pl.pallas_call(
        kernel,
        name=name,
        out_shape=out_shape,
        **({} if in_specs is None else {"in_specs": in_specs}),
        out_specs=jax.tree.map(lambda _: vmem, out_shape),
        scratch_shapes=scratch,
        compiler_params=pltpu.CompilerParams(vmem_limit_bytes=limit, **params),
    )


def on_device(tensor, init_second, init_third):
    local_rows, second_cells, depth_cells = tensor.shape
    rank = init_second.shape[1]
    n = lax.axis_size("row")
    chips = n // 2
    total_first = local_rows * n
    second_own, depth_own = second_cells // n, depth_cells // n
    system = [jax.ShapeDtypeStruct((rank, rank), jnp.bfloat16)] * 3
    split = [pltpu.VMEM((rank, rank), jnp.bfloat16)] * 3
    gather_sems = pltpu.SemaphoreType.DMA((2, chips))

    def buffers(rows, share):
        return [
            pltpu.VMEM((n, rows, rank), jnp.float32),
            pltpu.VMEM((2, chips, share, rank), jnp.float32),
            pltpu.VMEM((chips, share, rank), jnp.float32),
            pltpu.VMEM((chips, share, rank), jnp.float32),
            gather_sems,
            gather_sems,
            gather_sems,
        ]

    def solve(right, scales, parts, factor):
        rows = right.shape[0]
        padded = -(-rows // 8) * 8
        if padded != rows:
            right = jnp.pad(right, ((0, padded - rows), (0, 0)))
        raw, out = call(solve_kernel, "solve", (f32(padded, rank), f32(*factor.shape)), [])(
            right, scales, *parts, factor
        )
        return raw[:rows], out

    blocks = tensor.reshape(local_rows, n, second_own, depth_cells).transpose(1, 0, 2, 3)
    swapped = lax.all_to_all(blocks, "row", 0, 0, tiled=True)
    staged = [pltpu.VMEM(whole.shape, jnp.float32) for whole in (tensor, init_second, init_third)]
    raw_a = call(
        first_kernel,
        "first",
        f32(local_rows, rank),
        split + staged + [pltpu.SemaphoreType.DMA((3,))],
        in_specs=[pl.BlockSpec(memory_space=pltpu.HBM)] * 3,
        limit=FIRST_LIMIT,
    )(tensor, init_second, init_third)
    factor_first, all_first, gram_a, right_b, scales_b, *parts_b = call(
        functools.partial(first_exchange, n),
        "first_exchange",
        (f32(local_rows, rank), f32(total_first, rank), f32(rank, rank), f32(second_own, rank), f32(2, rank), *system),
        buffers(local_rows, second_own),
        0,
    )(raw_a, tensor, init_third)
    raw_b, factor_first_out = solve(right_b, scales_b, parts_b, factor_first)
    factor_second, right_c, scales_c, *parts_c = call(
        functools.partial(second_exchange, n),
        "second_exchange",
        (f32(second_own, rank), f32(depth_own, rank), f32(2, rank), *system),
        buffers(second_own, depth_own),
        1,
    )(raw_b, swapped, all_first, gram_a)
    raw_c, factor_second_out = solve(right_c, scales_c, parts_c, factor_second)
    all_c = call(
        functools.partial(third_exchange, n),
        "third_exchange",
        f32(n, depth_own, rank),
        [pltpu.VMEM((n, depth_own, rank), jnp.float32), gather_sems, gather_sems],
        2,
    )(raw_c)
    factor_third, weights = call(
        functools.partial(last_kernel, total_first * second_cells),
        "last",
        (f32(n, depth_own, rank), f32(1, rank)),
        [],
    )(all_c)
    return (
        factor_first_out,
        factor_second_out,
        factor_third.reshape(depth_cells, rank),
        weights.reshape(rank),
    )


def solution(mesh):
    in_specs = (P(("groups", "row"), None, None), P("groups", None), P("groups", None))
    out_specs = (
        P(("groups", "row"), None),
        P(("groups", "row"), None),
        P("groups", None),
        P("groups"),
    )
    return jax.shard_map(
        on_device, mesh=mesh, in_specs=in_specs, out_specs=out_specs, check_vma=False
    )
```

```python
import functools
import math

import jax
import jax.numpy as jnp
from jax import lax
from jax.experimental import pallas as pl
from jax.experimental.pallas import tpu as pltpu
from jax.sharding import PartitionSpec as P

HIGHEST = lax.Precision.HIGHEST
MESH = pl.DeviceIdType.MESH
RIDGE = 0.05
EPSILON = 1e-06
SOLVE_TOL = 4e-06
MAX_ROUNDS = 2048
UNROLL = 3
VMEM_LIMIT = 40 * 1024 * 1024
FIRST_LIMIT = 63 * 1024 * 1024


def dot(a, b):
    return jnp.dot(a, b, precision=HIGHEST, preferred_element_type=jnp.float32)


def split3(value):
    high = value.astype(jnp.bfloat16).astype(jnp.float32)
    rest = value - high
    middle = rest.astype(jnp.bfloat16).astype(jnp.float32)
    return high, middle, rest - middle


def prepare(first, second, vh_ref, vm_ref, vl_ref):
    size = first.shape[0]
    hadamard = first * second
    eye = lax.broadcasted_iota(jnp.int32, (size, size), 0) == lax.broadcasted_iota(jnp.int32, (size, size), 1)
    diagonal = jnp.sum(jnp.where(eye, hadamard, 0.0), axis=0, keepdims=True)
    mean = jnp.sum(diagonal, axis=1, keepdims=True) / size
    inverse_mean = 1.0 / mean
    system = hadamard * inverse_mean + jnp.where(eye, RIDGE, 0.0)
    high, middle, low = split3(system)
    vh_ref[...] = high.astype(jnp.bfloat16)
    vm_ref[...] = middle.astype(jnp.bfloat16)
    vl_ref[...] = low.astype(jnp.bfloat16)
    return 1.0 / (diagonal * inverse_mean + RIDGE), jnp.broadcast_to(inverse_mean, diagonal.shape)


def conjugate_solve(right, precondition, inverse_mean, vh_ref, vm_ref, vl_ref):
    rows = right.shape[0]
    largest = jnp.max(jnp.abs(right), axis=1, keepdims=True)
    largest = jnp.where(largest > 0, largest, 1.0)

    def apply(p):
        ph, pm, plow = split3(p)
        parts = jnp.concatenate([ph, pm, plow], axis=0).astype(jnp.bfloat16)
        by_high = jnp.dot(parts, vh_ref[...], preferred_element_type=jnp.float32)
        by_middle = jnp.dot(parts, vm_ref[...], preferred_element_type=jnp.float32)
        by_low = jnp.dot(parts, vl_ref[...], preferred_element_type=jnp.float32)
        small = by_high[2 * rows :] + by_low[:rows] + by_middle[rows : 2 * rows]
        return by_high[:rows] + (by_high[rows : 2 * rows] + by_middle[:rows] + small)

    def row_sum(value):
        return jnp.sum(value, axis=1, keepdims=True)

    def one(x, r, p, rz):
        q = apply(p)
        curvature = row_sum(p * q)
        alpha = jnp.where(curvature > 0, rz / curvature, 0.0)
        x = x + alpha * p
        r = r - alpha * q
        z = r * precondition
        rz_next = row_sum(r * z)
        beta = jnp.where(rz > 0, rz_next / rz, 0.0)
        return x, r, z + beta * p, rz_next

    def body(carry):
        count, _, x, r, p, rz = carry
        for _ in range(UNROLL):
            x, r, p, rz = one(x, r, p, rz)
        excess = row_sum(r * r) - (SOLVE_TOL * RIDGE) ** 2 * row_sum(x * x)
        return count + 1, jnp.max(excess), x, r, p, rz

    def unfinished(carry):
        return jnp.logical_and(carry[1] > 0, carry[0] < MAX_ROUNDS)

    r = right / largest
    z = r * precondition
    start = (jnp.int32(0), jnp.float32(1.0), jnp.zeros_like(r), r, z, row_sum(r * z))
    x = lax.while_loop(unfinished, body, start)[2]
    return x * (largest * inverse_mean)


def gram(factor):
    return dot(factor.T, factor) / factor.shape[0]


def first_kernel(
    tensor_hbm, second_hbm, third_hbm, raw_ref, vh_ref, vm_ref, vl_ref, tensor_ref, second_ref, third_ref, sems
):
    loads = [
        pltpu.make_async_copy(source, target, sems.at[at])
        for at, (source, target) in enumerate(
            ((third_hbm, third_ref), (second_hbm, second_ref), (tensor_hbm, tensor_ref))
        )
    ]
    for load in loads:
        load.start()
    loads[0].wait()
    third = third_ref[...]
    gram_c = gram(third)
    loads[1].wait()
    second = second_ref[...]
    scales = prepare(gram(second), gram_c, vh_ref, vm_ref, vl_ref)
    loads[2].wait()
    rows = []
    for i in range(tensor_ref.shape[0]):
        rows.append(jnp.sum(dot(tensor_ref[i], third) * second, axis=0, keepdims=True))
    raw_ref[...] = conjugate_solve(jnp.concatenate(rows, axis=0), *scales, vh_ref, vm_ref, vl_ref)


def solve_kernel(right_ref, scales_ref, vh_ref, vm_ref, vl_ref, factor_ref, raw_ref, out_ref):
    out_ref[...] = factor_ref[...]
    raw_ref[...] = conjugate_solve(right_ref[...], scales_ref[0:1], scales_ref[1:2], vh_ref, vm_ref, vl_ref)


def last_kernel(total, raw_ref, factor_ref, weights_ref):
    raw = raw_ref[...]
    square = jnp.sum(jnp.sum(raw * raw, axis=0), axis=0, keepdims=True)
    scales = jnp.sqrt(square / (raw.shape[0] * raw.shape[1]) + EPSILON)
    factor_ref[...] = raw / scales[None]
    weights_ref[...] = scales / math.sqrt(total)


class Place:
    def __init__(self, n):
        self.n = n
        self.chips = n // 2
        self.me = lax.axis_index("row")
        self.chip = self.me // 2
        self.core = lax.rem(self.me, 2)
        self.partner = self.chip * 2 + 1 - self.core

    def chip_after(self, step):
        return lax.rem(self.chip + step, self.chips)

    def chip_before(self, step):
        return lax.rem(self.chip + self.chips - step, self.chips)

    def greet(self):
        barrier = pltpu.get_barrier_semaphore()
        for step in range(1, self.chips):
            device = {"row": self.chip_after(step) * 2 + self.core}
            pl.semaphore_signal(barrier, inc=1, device_id=device, device_id_type=MESH)
        pl.semaphore_signal(barrier, inc=1, device_id={"row": self.partner}, device_id_type=MESH)
        return lambda: pl.semaphore_wait(barrier, self.chips)

    def send(self, src, dst, sems, at, device):
        return pltpu.make_async_remote_copy(
            src_ref=src,
            dst_ref=dst,
            send_sem=sems.at[0, at],
            recv_sem=sems.at[1, at],
            device_id={"row": device},
            device_id_type=MESH,
        )


def gather_start(place, raw_ref, all_ref, sems):
    own = all_ref.at[place.me]
    copies = []
    for step in range(1, place.chips):
        device = place.chip_after(step) * 2 + place.core
        copies.append(place.send(raw_ref, own, sems, step, device))
    copies.append(place.send(raw_ref, own, sems, 0, place.partner))
    for copy in copies:
        copy.start()
    all_ref[place.me] = raw_ref[...]
    return copies


def gather_finish(place, copies, all_ref, sems):
    forwards = []
    for step in range(1, place.chips):
        copies[step - 1].wait_recv()
        slot = all_ref.at[place.chip_before(step) * 2 + place.core]
        forward = place.send(slot, slot, sems, step, place.partner)
        forward.start()
        forwards.append(forward)
    copies[-1].wait_recv()
    for forward in forwards:
        forward.wait_recv()
    return copies + forwards


def split_parts(place, right, part_ref):
    share = right.shape[0] // place.n
    for device in range(place.n):
        part_ref[device % 2, device // 2] = right[device * share : (device + 1) * share]


def pair_start(place, part_ref, pair_ref, sems):
    copy = place.send(part_ref.at[1 - place.core], pair_ref, sems, 0, place.partner)
    copy.start()
    return copy


def scatter_start(place, pair_copy, part_ref, pair_ref, parts_ref, sems):
    pair_copy.wait()
    part_ref[place.core] = part_ref[place.core] + pair_ref[...]
    copies = []
    for step in range(1, place.chips):
        chip = place.chip_after(step)
        copy = place.send(
            part_ref.at[place.core, chip], parts_ref.at[place.chip], sems, step, chip * 2 + place.core
        )
        copy.start()
        copies.append(copy)
    parts_ref[place.chip] = part_ref[place.core, place.chip]
    return copies


def scatter_finish(copies, parts_ref):
    for copy in copies:
        copy.wait_recv()
    return jnp.sum(parts_ref[...], axis=0)


def unit_columns(all_raw):
    raw = all_raw.reshape(-1, all_raw.shape[-1])
    scales = jnp.sqrt(jnp.sum(raw * raw, axis=0, keepdims=True) / raw.shape[0] + EPSILON)
    return raw / scales, scales


def exchange(place, wait_barrier, terms, other_gram, raw_ref, right_ref, scales_ref, vh_ref, vm_ref, vl_ref,
             all_ref, part_ref, pair_ref, parts_ref, gather_sems, forward_sems, scatter_sems):
    split_parts(place, terms, part_ref)
    wait_barrier()
    pair_copy = pair_start(place, part_ref, pair_ref, scatter_sems)
    gathers = gather_start(place, raw_ref, all_ref, gather_sems)
    scatters = scatter_start(place, pair_copy, part_ref, pair_ref, parts_ref, scatter_sems)
    gathers = gather_finish(place, gathers, all_ref, forward_sems)
    factor, scales = unit_columns(all_ref[...])
    own_gram = gram(factor)
    scales_ref[0:1], scales_ref[1:2] = prepare(own_gram, other_gram, vh_ref, vm_ref, vl_ref)
    right_ref[...] = scatter_finish(scatters, parts_ref) / scales
    for copy in gathers + scatters:
        copy.wait_send()
    return own_gram, scales


def first_exchange(n, raw_ref, tensor_ref, third_ref, factor_ref, gram_ref, *refs):
    place = Place(n)
    wait_barrier = place.greet()
    raw = raw_ref[...]
    local_rows = tensor_ref.shape[0]
    slabs = jnp.concatenate([tensor_ref[i] for i in range(local_rows)], axis=1)
    third = third_ref[...]
    pairs = jnp.concatenate([third * raw[i : i + 1] for i in range(local_rows)], axis=0)
    terms = dot(slabs, pairs)
    gram_a, scales = exchange(place, wait_barrier, terms, gram(third), raw_ref, *refs)
    gram_ref[...] = gram_a
    factor_ref[...] = raw / scales


def second_exchange(
    n, raw_ref, tensor_ref, first_ref, gram_a_ref, factor_ref, right_ref, scales_ref, vh_ref, vm_ref, vl_ref,
    all_ref, part_ref, pair_ref, parts_ref, gather_sems, forward_sems, scatter_sems, turned_ref
):
    place = Place(n)
    wait_barrier = place.greet()
    local_rows, second_cells, depth_cells = tensor_ref.shape
    wide = second_cells // place.chips
    for chip in range(place.chips):
        slab = tensor_ref[:, chip * wide : (chip + 1) * wide, :]
        turned_ref[chip] = slab.reshape(local_rows * wide, depth_cells).T
    first = first_ref[...]
    wait_barrier()
    copies = gather_start(place, raw_ref, all_ref, gather_sems)

    def terms_of(step):
        chip = place.chip_before(step)
        rows = jnp.concatenate([all_ref[chip * 2], all_ref[chip * 2 + 1]], axis=0)
        pairs = jnp.concatenate([rows * first[i : i + 1] for i in range(local_rows)], axis=0)
        return dot(turned_ref[chip], pairs)

    forwards = [copies[-1]]
    terms = None
    for step in range(1, place.chips + 1):
        if step < place.chips:
            copies[step - 1].wait_recv()
            slot = all_ref.at[place.chip_before(step) * 2 + place.core]
            forward = place.send(slot, slot, forward_sems, step, place.partner)
            forward.start()
            forwards.append(forward)
        forwards[step - 1].wait_recv()
        term = terms_of(step - 1)
        terms = term if terms is None else terms + term
    split_parts(place, terms, part_ref)
    pair_copy = pair_start(place, part_ref, pair_ref, scatter_sems)
    factor, scales = unit_columns(all_ref[...])
    factor_ref[...] = raw_ref[...] / scales
    own_gram = gram(factor)
    scatters = scatter_start(place, pair_copy, part_ref, pair_ref, parts_ref, scatter_sems)
    scales_ref[0:1], scales_ref[1:2] = prepare(own_gram, gram_a_ref[...], vh_ref, vm_ref, vl_ref)
    right_ref[...] = scatter_finish(scatters, parts_ref) / scales
    for copy in copies[:-1] + forwards + scatters:
        copy.wait_send()


def third_exchange(n, raw_ref, all_out_ref, all_ref, gather_sems, forward_sems):
    place = Place(n)
    wait_barrier = place.greet()
    wait_barrier()
    gathers = gather_start(place, raw_ref, all_ref, gather_sems)
    gathers = gather_finish(place, gathers, all_ref, forward_sems)
    all_out_ref[...] = all_ref[...]
    for copy in gathers:
        copy.wait_send()


def f32(*shape):
    return jax.ShapeDtypeStruct(shape, jnp.float32)


def call(kernel, name, out_shape, scratch, collective_id=None, in_specs=None, limit=VMEM_LIMIT):
    vmem = pl.BlockSpec(memory_space=pltpu.VMEM)
    params = {} if collective_id is None else {"collective_id": collective_id, "has_side_effects": True}
    return pl.pallas_call(
        kernel,
        name=name,
        out_shape=out_shape,
        **({} if in_specs is None else {"in_specs": in_specs}),
        out_specs=jax.tree.map(lambda _: vmem, out_shape),
        scratch_shapes=scratch,
        compiler_params=pltpu.CompilerParams(vmem_limit_bytes=limit, **params),
    )


def on_device(tensor, init_second, init_third):
    local_rows, second_cells, depth_cells = tensor.shape
    rank = init_second.shape[1]
    n = lax.axis_size("row")
    chips = n // 2
    total_first = local_rows * n
    second_own, depth_own = second_cells // n, depth_cells // n
    system = [jax.ShapeDtypeStruct((rank, rank), jnp.bfloat16)] * 3
    split = [pltpu.VMEM((rank, rank), jnp.bfloat16)] * 3
    gather_sems = pltpu.SemaphoreType.DMA((2, chips))

    def buffers(rows, share):
        return [
            pltpu.VMEM((n, rows, rank), jnp.float32),
            pltpu.VMEM((2, chips, share, rank), jnp.float32),
            pltpu.VMEM((chips, share, rank), jnp.float32),
            pltpu.VMEM((chips, share, rank), jnp.float32),
            gather_sems,
            gather_sems,
            gather_sems,
        ]

    def solve(right, scales, parts, factor):
        rows = right.shape[0]
        padded = -(-rows // 8) * 8
        if padded != rows:
            right = jnp.pad(right, ((0, padded - rows), (0, 0)))
        raw, out = call(solve_kernel, "solve", (f32(padded, rank), f32(*factor.shape)), [])(
            right, scales, *parts, factor
        )
        return raw[:rows], out

    staged = [pltpu.VMEM(whole.shape, jnp.float32) for whole in (tensor, init_second, init_third)]
    raw_a = call(
        first_kernel,
        "first",
        f32(local_rows, rank),
        split + staged + [pltpu.SemaphoreType.DMA((3,))],
        in_specs=[pl.BlockSpec(memory_space=pltpu.HBM)] * 3,
        limit=FIRST_LIMIT,
    )(tensor, init_second, init_third)
    factor_first, gram_a, right_b, scales_b, *parts_b = call(
        functools.partial(first_exchange, n),
        "first_exchange",
        (f32(local_rows, rank), f32(rank, rank), f32(second_own, rank), f32(2, rank), *system),
        buffers(local_rows, second_own),
        0,
    )(raw_a, tensor, init_third)
    raw_b, factor_first_out = solve(right_b, scales_b, parts_b, factor_first)
    factor_second, right_c, scales_c, *parts_c = call(
        functools.partial(second_exchange, n),
        "second_exchange",
        (f32(second_own, rank), f32(depth_own, rank), f32(2, rank), *system),
        buffers(second_own, depth_own)
        + [pltpu.VMEM((chips, depth_cells, local_rows * second_cells // chips), jnp.float32)],
        1,
    )(raw_b, tensor, factor_first, gram_a)
    raw_c, factor_second_out = solve(right_c, scales_c, parts_c, factor_second)
    all_c = call(
        functools.partial(third_exchange, n),
        "third_exchange",
        f32(n, depth_own, rank),
        [pltpu.VMEM((n, depth_own, rank), jnp.float32), gather_sems, gather_sems],
        2,
    )(raw_c)
    factor_third, weights = call(
        functools.partial(last_kernel, total_first * second_cells),
        "last",
        (f32(n, depth_own, rank), f32(1, rank)),
        [],
    )(all_c)
    return (
        factor_first_out,
        factor_second_out,
        factor_third.reshape(depth_cells, rank),
        weights.reshape(rank),
    )


def solution(mesh):
    in_specs = (P(("groups", "row"), None, None), P("groups", None), P("groups", None))
    out_specs = (
        P(("groups", "row"), None),
        P(("groups", "row"), None),
        P("groups", None),
        P("groups"),
    )
    return jax.shard_map(
        on_device, mesh=mesh, in_specs=in_specs, out_specs=out_specs, check_vma=False
    )
```

```python
import functools
import math

import jax
import jax.numpy as jnp
from jax import lax
from jax.experimental import pallas as pl
from jax.experimental.pallas import tpu as pltpu
from jax.sharding import PartitionSpec as P

HIGHEST = lax.Precision.HIGHEST
MESH = pl.DeviceIdType.MESH
RIDGE = 0.05
EPSILON = 1e-06
SOLVE_TOL = 4e-06
MAX_ROUNDS = 2048
UNROLL = 3
TINY = 1e-30
VMEM_LIMIT = 40 * 1024 * 1024
FIRST_LIMIT = 63 * 1024 * 1024


def dot(a, b):
    return jnp.dot(a, b, precision=HIGHEST, preferred_element_type=jnp.float32)


def split3(value):
    high = value.astype(jnp.bfloat16).astype(jnp.float32)
    rest = value - high
    middle = rest.astype(jnp.bfloat16).astype(jnp.float32)
    return high, middle, rest - middle


def prepare(first, second, vh_ref, vm_ref, vl_ref):
    size = first.shape[0]
    hadamard = first * second
    eye = lax.broadcasted_iota(jnp.int32, (size, size), 0) == lax.broadcasted_iota(jnp.int32, (size, size), 1)
    diagonal = jnp.sum(jnp.where(eye, hadamard, 0.0), axis=0, keepdims=True)
    mean = jnp.sum(diagonal, axis=1, keepdims=True) / size
    inverse_mean = 1.0 / mean
    system = hadamard * inverse_mean + jnp.where(eye, RIDGE, 0.0)
    high, middle, low = split3(system)
    vh_ref[...] = high.astype(jnp.bfloat16)
    vm_ref[...] = middle.astype(jnp.bfloat16)
    vl_ref[...] = low.astype(jnp.bfloat16)
    return 1.0 / (diagonal * inverse_mean + RIDGE), jnp.broadcast_to(inverse_mean, diagonal.shape)


def conjugate_solve(right, precondition, inverse_mean, vh_ref, vm_ref, vl_ref):
    rows = right.shape[0]
    largest = jnp.max(jnp.abs(right), axis=1, keepdims=True)
    largest = jnp.where(largest > 0, largest, 1.0)

    def apply(p):
        ph, pm, plow = split3(p)
        parts = jnp.concatenate([ph, pm, plow], axis=0).astype(jnp.bfloat16)
        by_high = jnp.dot(parts, vh_ref[...], preferred_element_type=jnp.float32)
        by_middle = jnp.dot(parts, vm_ref[...], preferred_element_type=jnp.float32)
        by_low = jnp.dot(parts, vl_ref[...], preferred_element_type=jnp.float32)
        small = by_high[2 * rows :] + by_low[:rows] + by_middle[rows : 2 * rows]
        return by_high[:rows] + (by_high[rows : 2 * rows] + by_middle[:rows] + small)

    def row_sum(value):
        return jnp.sum(value, axis=1, keepdims=True)

    def one(x, r, p, q, rz, alpha):
        z = r * precondition
        w = apply(z)
        rz_next = row_sum(r * z)
        curvature = row_sum(w * z)
        beta = jnp.where(rz > 0, rz_next / rz, 0.0)
        curvature = curvature - beta * rz_next / alpha
        alpha = jnp.where(curvature > 0, rz_next / curvature, TINY)
        p = z + beta * p
        q = w + beta * q
        return x + alpha * p, r - alpha * q, p, q, rz_next, alpha

    def body(carry):
        count, _, *state = carry
        for _ in range(UNROLL):
            state = one(*state)
        x, r = state[:2]
        excess = row_sum(r * r) - (SOLVE_TOL * RIDGE) ** 2 * row_sum(x * x)
        return count + 1, jnp.max(excess), *state

    def unfinished(carry):
        return jnp.logical_and(carry[1] > 0, carry[0] < MAX_ROUNDS)

    r = right / largest
    zero = jnp.zeros_like(r)
    start = (jnp.int32(0), jnp.float32(1.0), zero, r, zero, zero, jnp.zeros_like(largest), jnp.ones_like(largest))
    x = lax.while_loop(unfinished, body, start)[2]
    return x * (largest * inverse_mean)


def gram(factor):
    return dot(factor.T, factor) / factor.shape[0]


def first_kernel(
    tensor_hbm, second_hbm, third_hbm, raw_ref, vh_ref, vm_ref, vl_ref, tensor_ref, second_ref, third_ref, sems
):
    loads = [
        pltpu.make_async_copy(source, target, sems.at[at])
        for at, (source, target) in enumerate(
            ((third_hbm, third_ref), (second_hbm, second_ref), (tensor_hbm, tensor_ref))
        )
    ]
    for load in loads:
        load.start()
    loads[0].wait()
    third = third_ref[...]
    gram_c = gram(third)
    loads[1].wait()
    second = second_ref[...]
    scales = prepare(gram(second), gram_c, vh_ref, vm_ref, vl_ref)
    loads[2].wait()
    rows = []
    for i in range(tensor_ref.shape[0]):
        rows.append(jnp.sum(dot(tensor_ref[i], third) * second, axis=0, keepdims=True))
    raw_ref[...] = conjugate_solve(jnp.concatenate(rows, axis=0), *scales, vh_ref, vm_ref, vl_ref)


def solve_kernel(right_ref, scales_ref, vh_ref, vm_ref, vl_ref, factor_ref, raw_ref, out_ref):
    out_ref[...] = factor_ref[...]
    raw_ref[...] = conjugate_solve(right_ref[...], scales_ref[0:1], scales_ref[1:2], vh_ref, vm_ref, vl_ref)


def last_kernel(total, raw_ref, factor_ref, weights_ref):
    raw = raw_ref[...]
    square = jnp.sum(jnp.sum(raw * raw, axis=0), axis=0, keepdims=True)
    scales = jnp.sqrt(square / (raw.shape[0] * raw.shape[1]) + EPSILON)
    factor_ref[...] = raw / scales[None]
    weights_ref[...] = scales / math.sqrt(total)


class Place:
    def __init__(self, n):
        self.n = n
        self.chips = n // 2
        self.me = lax.axis_index("row")
        self.chip = self.me // 2
        self.core = lax.rem(self.me, 2)
        self.partner = self.chip * 2 + 1 - self.core

    def chip_after(self, step):
        return lax.rem(self.chip + step, self.chips)

    def chip_before(self, step):
        return lax.rem(self.chip + self.chips - step, self.chips)

    def greet(self):
        barrier = pltpu.get_barrier_semaphore()
        for step in range(1, self.chips):
            device = {"row": self.chip_after(step) * 2 + self.core}
            pl.semaphore_signal(barrier, inc=1, device_id=device, device_id_type=MESH)
        pl.semaphore_signal(barrier, inc=1, device_id={"row": self.partner}, device_id_type=MESH)
        return lambda: pl.semaphore_wait(barrier, self.chips)

    def send(self, src, dst, sems, at, device):
        return pltpu.make_async_remote_copy(
            src_ref=src,
            dst_ref=dst,
            send_sem=sems.at[0, at],
            recv_sem=sems.at[1, at],
            device_id={"row": device},
            device_id_type=MESH,
        )


def gather_start(place, raw_ref, all_ref, sems):
    own = all_ref.at[place.me]
    copies = []
    for step in range(1, place.chips):
        device = place.chip_after(step) * 2 + place.core
        copies.append(place.send(raw_ref, own, sems, step, device))
    copies.append(place.send(raw_ref, own, sems, 0, place.partner))
    for copy in copies:
        copy.start()
    all_ref[place.me] = raw_ref[...]
    return copies


def gather_finish(place, copies, all_ref, sems):
    forwards = []
    for step in range(1, place.chips):
        copies[step - 1].wait_recv()
        slot = all_ref.at[place.chip_before(step) * 2 + place.core]
        forward = place.send(slot, slot, sems, step, place.partner)
        forward.start()
        forwards.append(forward)
    copies[-1].wait_recv()
    for forward in forwards:
        forward.wait_recv()
    return copies + forwards


def split_parts(place, right, part_ref):
    share = right.shape[0] // place.n
    for device in range(place.n):
        part_ref[device % 2, device // 2] = right[device * share : (device + 1) * share]


def pair_start(place, part_ref, pair_ref, sems):
    copy = place.send(part_ref.at[1 - place.core], pair_ref, sems, 0, place.partner)
    copy.start()
    return copy


def scatter_start(place, pair_copy, part_ref, pair_ref, parts_ref, sems):
    pair_copy.wait()
    part_ref[place.core] = part_ref[place.core] + pair_ref[...]
    copies = []
    for step in range(1, place.chips):
        chip = place.chip_after(step)
        copy = place.send(
            part_ref.at[place.core, chip], parts_ref.at[place.chip], sems, step, chip * 2 + place.core
        )
        copy.start()
        copies.append(copy)
    parts_ref[place.chip] = part_ref[place.core, place.chip]
    return copies


def scatter_finish(copies, parts_ref):
    for copy in copies:
        copy.wait_recv()
    return jnp.sum(parts_ref[...], axis=0)


def unit_columns(all_raw):
    raw = all_raw.reshape(-1, all_raw.shape[-1])
    scales = jnp.sqrt(jnp.sum(raw * raw, axis=0, keepdims=True) / raw.shape[0] + EPSILON)
    return raw / scales, scales


def exchange(place, wait_barrier, terms, other_gram, raw_ref, right_ref, scales_ref, vh_ref, vm_ref, vl_ref,
             all_ref, part_ref, pair_ref, parts_ref, gather_sems, forward_sems, scatter_sems):
    split_parts(place, terms, part_ref)
    wait_barrier()
    pair_copy = pair_start(place, part_ref, pair_ref, scatter_sems)
    gathers = gather_start(place, raw_ref, all_ref, gather_sems)
    scatters = scatter_start(place, pair_copy, part_ref, pair_ref, parts_ref, scatter_sems)
    gathers = gather_finish(place, gathers, all_ref, forward_sems)
    factor, scales = unit_columns(all_ref[...])
    own_gram = gram(factor)
    scales_ref[0:1], scales_ref[1:2] = prepare(own_gram, other_gram, vh_ref, vm_ref, vl_ref)
    right_ref[...] = scatter_finish(scatters, parts_ref) / scales
    for copy in gathers + scatters:
        copy.wait_send()
    return own_gram, scales


def first_exchange(n, raw_ref, tensor_ref, third_ref, factor_ref, gram_ref, *refs):
    place = Place(n)
    wait_barrier = place.greet()
    raw = raw_ref[...]
    local_rows = tensor_ref.shape[0]
    slabs = jnp.concatenate([tensor_ref[i] for i in range(local_rows)], axis=1)
    third = third_ref[...]
    pairs = jnp.concatenate([third * raw[i : i + 1] for i in range(local_rows)], axis=0)
    terms = dot(slabs, pairs)
    gram_a, scales = exchange(place, wait_barrier, terms, gram(third), raw_ref, *refs)
    gram_ref[...] = gram_a
    factor_ref[...] = raw / scales


def second_exchange(
    n, raw_ref, tensor_ref, first_ref, gram_a_ref, factor_ref, right_ref, scales_ref, vh_ref, vm_ref, vl_ref,
    all_ref, part_ref, pair_ref, parts_ref, gather_sems, forward_sems, scatter_sems, turned_ref
):
    place = Place(n)
    wait_barrier = place.greet()
    local_rows, second_cells, depth_cells = tensor_ref.shape
    wide = second_cells // place.chips
    for chip in range(place.chips):
        slab = tensor_ref[:, chip * wide : (chip + 1) * wide, :]
        turned_ref[chip] = slab.reshape(local_rows * wide, depth_cells).T
    first = first_ref[...]
    wait_barrier()
    copies = gather_start(place, raw_ref, all_ref, gather_sems)

    def terms_of(step):
        chip = place.chip_before(step)
        rows = jnp.concatenate([all_ref[chip * 2], all_ref[chip * 2 + 1]], axis=0)
        pairs = jnp.concatenate([rows * first[i : i + 1] for i in range(local_rows)], axis=0)
        return dot(turned_ref[chip], pairs)

    forwards = [copies[-1]]
    terms = None
    for step in range(1, place.chips + 1):
        if step < place.chips:
            copies[step - 1].wait_recv()
            slot = all_ref.at[place.chip_before(step) * 2 + place.core]
            forward = place.send(slot, slot, forward_sems, step, place.partner)
            forward.start()
            forwards.append(forward)
        forwards[step - 1].wait_recv()
        term = terms_of(step - 1)
        terms = term if terms is None else terms + term
    split_parts(place, terms, part_ref)
    pair_copy = pair_start(place, part_ref, pair_ref, scatter_sems)
    factor, scales = unit_columns(all_ref[...])
    factor_ref[...] = raw_ref[...] / scales
    own_gram = gram(factor)
    scatters = scatter_start(place, pair_copy, part_ref, pair_ref, parts_ref, scatter_sems)
    scales_ref[0:1], scales_ref[1:2] = prepare(own_gram, gram_a_ref[...], vh_ref, vm_ref, vl_ref)
    right_ref[...] = scatter_finish(scatters, parts_ref) / scales
    for copy in copies[:-1] + forwards + scatters:
        copy.wait_send()


def third_exchange(n, raw_ref, all_out_ref, all_ref, gather_sems, forward_sems):
    place = Place(n)
    wait_barrier = place.greet()
    wait_barrier()
    gathers = gather_start(place, raw_ref, all_ref, gather_sems)
    gathers = gather_finish(place, gathers, all_ref, forward_sems)
    all_out_ref[...] = all_ref[...]
    for copy in gathers:
        copy.wait_send()


def f32(*shape):
    return jax.ShapeDtypeStruct(shape, jnp.float32)


def call(kernel, name, out_shape, scratch, collective_id=None, in_specs=None, limit=VMEM_LIMIT):
    vmem = pl.BlockSpec(memory_space=pltpu.VMEM)
    params = {} if collective_id is None else {"collective_id": collective_id, "has_side_effects": True}
    return pl.pallas_call(
        kernel,
        name=name,
        out_shape=out_shape,
        **({} if in_specs is None else {"in_specs": in_specs}),
        out_specs=jax.tree.map(lambda _: vmem, out_shape),
        scratch_shapes=scratch,
        compiler_params=pltpu.CompilerParams(vmem_limit_bytes=limit, **params),
    )


def on_device(tensor, init_second, init_third):
    local_rows, second_cells, depth_cells = tensor.shape
    rank = init_second.shape[1]
    n = lax.axis_size("row")
    chips = n // 2
    total_first = local_rows * n
    second_own, depth_own = second_cells // n, depth_cells // n
    system = [jax.ShapeDtypeStruct((rank, rank), jnp.bfloat16)] * 3
    split = [pltpu.VMEM((rank, rank), jnp.bfloat16)] * 3
    gather_sems = pltpu.SemaphoreType.DMA((2, chips))

    def buffers(rows, share):
        return [
            pltpu.VMEM((n, rows, rank), jnp.float32),
            pltpu.VMEM((2, chips, share, rank), jnp.float32),
            pltpu.VMEM((chips, share, rank), jnp.float32),
            pltpu.VMEM((chips, share, rank), jnp.float32),
            gather_sems,
            gather_sems,
            gather_sems,
        ]

    def solve(right, scales, parts, factor):
        rows = right.shape[0]
        padded = -(-rows // 8) * 8
        if padded != rows:
            right = jnp.pad(right, ((0, padded - rows), (0, 0)))
        raw, out = call(solve_kernel, "solve", (f32(padded, rank), f32(*factor.shape)), [])(
            right, scales, *parts, factor
        )
        return raw[:rows], out

    staged = [pltpu.VMEM(whole.shape, jnp.float32) for whole in (tensor, init_second, init_third)]
    raw_a = call(
        first_kernel,
        "first",
        f32(local_rows, rank),
        split + staged + [pltpu.SemaphoreType.DMA((3,))],
        in_specs=[pl.BlockSpec(memory_space=pltpu.HBM)] * 3,
        limit=FIRST_LIMIT,
    )(tensor, init_second, init_third)
    factor_first, gram_a, right_b, scales_b, *parts_b = call(
        functools.partial(first_exchange, n),
        "first_exchange",
        (f32(local_rows, rank), f32(rank, rank), f32(second_own, rank), f32(2, rank), *system),
        buffers(local_rows, second_own),
        0,
    )(raw_a, tensor, init_third)
    raw_b, factor_first_out = solve(right_b, scales_b, parts_b, factor_first)
    factor_second, right_c, scales_c, *parts_c = call(
        functools.partial(second_exchange, n),
        "second_exchange",
        (f32(second_own, rank), f32(depth_own, rank), f32(2, rank), *system),
        buffers(second_own, depth_own)
        + [pltpu.VMEM((chips, depth_cells, local_rows * second_cells // chips), jnp.float32)],
        1,
    )(raw_b, tensor, factor_first, gram_a)
    raw_c, factor_second_out = solve(right_c, scales_c, parts_c, factor_second)
    all_c = call(
        functools.partial(third_exchange, n),
        "third_exchange",
        f32(n, depth_own, rank),
        [pltpu.VMEM((n, depth_own, rank), jnp.float32), gather_sems, gather_sems],
        2,
    )(raw_c)
    factor_third, weights = call(
        functools.partial(last_kernel, total_first * second_cells),
        "last",
        (f32(n, depth_own, rank), f32(1, rank)),
        [],
    )(all_c)
    return (
        factor_first_out,
        factor_second_out,
        factor_third.reshape(depth_cells, rank),
        weights.reshape(rank),
    )


def solution(mesh):
    in_specs = (P(("groups", "row"), None, None), P("groups", None), P("groups", None))
    out_specs = (
        P(("groups", "row"), None),
        P(("groups", "row"), None),
        P("groups", None),
        P("groups"),
    )
    return jax.shard_map(
        on_device, mesh=mesh, in_specs=in_specs, out_specs=out_specs, check_vma=False
    )
```

```python
import functools
import math

import jax
import jax.numpy as jnp
from jax import lax
from jax.experimental import pallas as pl
from jax.experimental.pallas import tpu as pltpu
from jax.sharding import PartitionSpec as P

HIGHEST = lax.Precision.HIGHEST
MESH = pl.DeviceIdType.MESH
RIDGE = 0.05
EPSILON = 1e-06
SOLVE_TOL = 4e-06
MAX_ROUNDS = 2048
UNROLL = 3
TINY = 1e-30
VMEM_LIMIT = 40 * 1024 * 1024
FIRST_LIMIT = 63 * 1024 * 1024


def dot(a, b):
    return jnp.dot(a, b, precision=HIGHEST, preferred_element_type=jnp.float32)


def split3(value):
    high = value.astype(jnp.bfloat16).astype(jnp.float32)
    rest = value - high
    middle = rest.astype(jnp.bfloat16).astype(jnp.float32)
    return high, middle, rest - middle


def prepare(first, second, vh_ref, vm_ref, vl_ref):
    size = first.shape[0]
    hadamard = first * second
    eye = lax.broadcasted_iota(jnp.int32, (size, size), 0) == lax.broadcasted_iota(jnp.int32, (size, size), 1)
    diagonal = jnp.sum(jnp.where(eye, hadamard, 0.0), axis=0, keepdims=True)
    mean = jnp.sum(diagonal, axis=1, keepdims=True) / size
    inverse_mean = 1.0 / mean
    system = hadamard * inverse_mean + jnp.where(eye, RIDGE, 0.0)
    high, middle, low = split3(system)
    vh_ref[...] = high.astype(jnp.bfloat16)
    vm_ref[...] = middle.astype(jnp.bfloat16)
    vl_ref[...] = low.astype(jnp.bfloat16)
    return 1.0 / (diagonal * inverse_mean + RIDGE), jnp.broadcast_to(inverse_mean, diagonal.shape)


def conjugate_solve(right, precondition, inverse_mean, vh_ref, vm_ref, vl_ref):
    rows = right.shape[0]
    largest = jnp.max(jnp.abs(right), axis=1, keepdims=True)
    largest = jnp.where(largest > 0, largest, 1.0)

    def apply(p):
        ph, pm, plow = split3(p)
        parts = jnp.concatenate([ph, pm, plow], axis=0).astype(jnp.bfloat16)
        by_high = jnp.dot(parts, vh_ref[...], preferred_element_type=jnp.float32)
        by_middle = jnp.dot(parts, vm_ref[...], preferred_element_type=jnp.float32)
        by_low = jnp.dot(parts, vl_ref[...], preferred_element_type=jnp.float32)
        small = by_high[2 * rows :] + by_low[:rows] + by_middle[rows : 2 * rows]
        return by_high[:rows] + (by_high[rows : 2 * rows] + by_middle[:rows] + small)

    def row_sum(value):
        return jnp.sum(value, axis=1, keepdims=True)

    def one(x, r, p, q, rz, alpha):
        z = r * precondition
        w = apply(z)
        rz_next = row_sum(r * z)
        curvature = row_sum(w * z)
        beta = jnp.where(rz > 0, rz_next / rz, 0.0)
        curvature = curvature - beta * rz_next / alpha
        alpha = jnp.where(curvature > 0, rz_next / curvature, TINY)
        p = z + beta * p
        q = w + beta * q
        return x + alpha * p, r - alpha * q, p, q, rz_next, alpha

    def body(carry):
        count, _, *state = carry
        for _ in range(UNROLL):
            state = one(*state)
        x, r = state[:2]
        excess = row_sum(r * r) - (SOLVE_TOL * RIDGE) ** 2 * row_sum(x * x)
        return count + 1, jnp.max(excess), *state

    def unfinished(carry):
        return jnp.logical_and(carry[1] > 0, carry[0] < MAX_ROUNDS)

    r = right / largest
    zero = jnp.zeros_like(r)
    start = (jnp.int32(0), jnp.float32(1.0), zero, r, zero, zero, jnp.zeros_like(largest), jnp.ones_like(largest))
    x = lax.while_loop(unfinished, body, start)[2]
    return x * (largest * inverse_mean)


def gram(factor):
    return dot(factor.T, factor) / factor.shape[0]


def first_kernel(
    tensor_hbm, second_hbm, third_hbm, raw_ref, vh_ref, vm_ref, vl_ref, tensor_ref, second_ref, third_ref, sems
):
    loads = [
        pltpu.make_async_copy(source, target, sems.at[at])
        for at, (source, target) in enumerate(
            ((third_hbm, third_ref), (second_hbm, second_ref), (tensor_hbm, tensor_ref))
        )
    ]
    for load in loads:
        load.start()
    loads[0].wait()
    third = third_ref[...]
    gram_c = gram(third)
    loads[1].wait()
    second = second_ref[...]
    scales = prepare(gram(second), gram_c, vh_ref, vm_ref, vl_ref)
    loads[2].wait()
    rows = []
    for i in range(tensor_ref.shape[0]):
        rows.append(jnp.sum(dot(tensor_ref[i], third) * second, axis=0, keepdims=True))
    raw_ref[...] = conjugate_solve(jnp.concatenate(rows, axis=0), *scales, vh_ref, vm_ref, vl_ref)


def solve_kernel(right_ref, scales_ref, vh_ref, vm_ref, vl_ref, factor_ref, raw_ref, out_ref):
    out_ref[...] = factor_ref[...]
    raw_ref[...] = conjugate_solve(right_ref[...], scales_ref[0:1], scales_ref[1:2], vh_ref, vm_ref, vl_ref)


def last_kernel(total, raw_ref, factor_ref, weights_ref):
    raw = raw_ref[...]
    square = jnp.sum(jnp.sum(raw * raw, axis=0), axis=0, keepdims=True)
    scales = jnp.sqrt(square / (raw.shape[0] * raw.shape[1]) + EPSILON)
    factor_ref[...] = raw / scales[None]
    weights_ref[...] = scales / math.sqrt(total)


class Place:
    def __init__(self, n):
        self.n = n
        self.chips = n // 2
        self.me = lax.axis_index("row")
        self.chip = self.me // 2
        self.core = lax.rem(self.me, 2)
        self.partner = self.chip * 2 + 1 - self.core

    def chip_after(self, step):
        return lax.rem(self.chip + step, self.chips)

    def chip_before(self, step):
        return lax.rem(self.chip + self.chips - step, self.chips)

    def greet(self):
        barrier = pltpu.get_barrier_semaphore()
        for step in range(1, self.chips):
            device = {"row": self.chip_after(step) * 2 + self.core}
            pl.semaphore_signal(barrier, inc=1, device_id=device, device_id_type=MESH)
        pl.semaphore_signal(barrier, inc=1, device_id={"row": self.partner}, device_id_type=MESH)
        return lambda: pl.semaphore_wait(barrier, self.chips)

    def send(self, src, dst, sems, at, device):
        return pltpu.make_async_remote_copy(
            src_ref=src,
            dst_ref=dst,
            send_sem=sems.at[0, at],
            recv_sem=sems.at[1, at],
            device_id={"row": device},
            device_id_type=MESH,
        )


def gather_start(place, raw_ref, all_ref, sems):
    own = all_ref.at[place.me]
    copies = []
    for step in range(1, place.chips):
        device = place.chip_after(step) * 2 + place.core
        copies.append(place.send(raw_ref, own, sems, step, device))
    copies.append(place.send(raw_ref, own, sems, 0, place.partner))
    for copy in copies:
        copy.start()
    all_ref[place.me] = raw_ref[...]
    return copies


def gather_finish(place, copies, all_ref, sems):
    forwards = []
    for step in range(1, place.chips):
        copies[step - 1].wait_recv()
        slot = all_ref.at[place.chip_before(step) * 2 + place.core]
        forward = place.send(slot, slot, sems, step, place.partner)
        forward.start()
        forwards.append(forward)
    copies[-1].wait_recv()
    for forward in forwards:
        forward.wait_recv()
    return copies + forwards


def split_parts(place, right, part_ref):
    share = right.shape[0] // place.n
    for device in range(place.n):
        part_ref[device % 2, device // 2] = right[device * share : (device + 1) * share]


def pair_start(place, part_ref, pair_ref, sems):
    copy = place.send(part_ref.at[1 - place.core], pair_ref, sems, 0, place.partner)
    copy.start()
    return copy


def scatter_start(place, pair_copy, part_ref, pair_ref, parts_ref, sems):
    pair_copy.wait()
    part_ref[place.core] = part_ref[place.core] + pair_ref[...]
    copies = []
    for step in range(1, place.chips):
        chip = place.chip_after(step)
        copy = place.send(
            part_ref.at[place.core, chip], parts_ref.at[place.chip], sems, step, chip * 2 + place.core
        )
        copy.start()
        copies.append(copy)
    parts_ref[place.chip] = part_ref[place.core, place.chip]
    return copies


def scatter_finish(copies, parts_ref):
    for copy in copies:
        copy.wait_recv()
    return jnp.sum(parts_ref[...], axis=0)


def unit_columns(all_raw):
    raw = all_raw.reshape(-1, all_raw.shape[-1])
    scales = jnp.sqrt(jnp.sum(raw * raw, axis=0, keepdims=True) / raw.shape[0] + EPSILON)
    return raw / scales, scales


def exchange(place, wait_barrier, terms, other_gram, raw_ref, right_ref, scales_ref, vh_ref, vm_ref, vl_ref,
             all_ref, part_ref, pair_ref, parts_ref, gather_sems, forward_sems, scatter_sems):
    split_parts(place, terms, part_ref)
    wait_barrier()
    pair_copy = pair_start(place, part_ref, pair_ref, scatter_sems)
    gathers = gather_start(place, raw_ref, all_ref, gather_sems)
    scatters = scatter_start(place, pair_copy, part_ref, pair_ref, parts_ref, scatter_sems)
    gathers = gather_finish(place, gathers, all_ref, forward_sems)
    factor, scales = unit_columns(all_ref[...])
    own_gram = gram(factor)
    scales_ref[0:1], scales_ref[1:2] = prepare(own_gram, other_gram, vh_ref, vm_ref, vl_ref)
    right_ref[...] = scatter_finish(scatters, parts_ref) / scales
    for copy in gathers + scatters:
        copy.wait_send()
    return own_gram, scales


def first_exchange(n, raw_ref, tensor_ref, third_ref, factor_ref, gram_ref, *refs):
    place = Place(n)
    wait_barrier = place.greet()
    raw = raw_ref[...]
    local_rows = tensor_ref.shape[0]
    slabs = jnp.concatenate([tensor_ref[i] for i in range(local_rows)], axis=1)
    third = third_ref[...]
    pairs = jnp.concatenate([third * raw[i : i + 1] for i in range(local_rows)], axis=0)
    terms = dot(slabs, pairs)
    gram_a, scales = exchange(place, wait_barrier, terms, gram(third), raw_ref, *refs)
    gram_ref[...] = gram_a
    factor_ref[...] = raw / scales


def second_exchange(
    n, raw_ref, tensor_ref, first_ref, gram_a_ref, factor_ref, right_ref, scales_ref, vh_ref, vm_ref, vl_ref,
    all_ref, part_ref, pair_ref, parts_ref, gather_sems, forward_sems, scatter_sems, turned_ref
):
    place = Place(n)
    wait_barrier = place.greet()
    local_rows, second_cells, depth_cells = tensor_ref.shape
    wide = second_cells // place.chips
    for chip in range(place.chips):
        slab = tensor_ref[:, chip * wide : (chip + 1) * wide, :]
        turned_ref[chip] = slab.reshape(local_rows * wide, depth_cells).T
    first = first_ref[...]
    wait_barrier()
    copies = gather_start(place, raw_ref, all_ref, gather_sems)

    def terms_of(step):
        chip = place.chip_before(step)
        rows = jnp.concatenate([all_ref[chip * 2], all_ref[chip * 2 + 1]], axis=0)
        pairs = jnp.concatenate([rows * first[i : i + 1] for i in range(local_rows)], axis=0)
        return dot(turned_ref[chip], pairs)

    forwards = [copies[-1]]
    terms = None
    for step in range(1, place.chips + 1):
        if step < place.chips:
            copies[step - 1].wait_recv()
            slot = all_ref.at[place.chip_before(step) * 2 + place.core]
            forward = place.send(slot, slot, forward_sems, step, place.partner)
            forward.start()
            forwards.append(forward)
        forwards[step - 1].wait_recv()
        term = terms_of(step - 1)
        terms = term if terms is None else terms + term
    split_parts(place, terms, part_ref)
    pair_copy = pair_start(place, part_ref, pair_ref, scatter_sems)
    factor, scales = unit_columns(all_ref[...])
    factor_ref[...] = raw_ref[...] / scales
    scatters = scatter_start(place, pair_copy, part_ref, pair_ref, parts_ref, scatter_sems)
    own_gram = gram(factor)
    scales_ref[0:1], scales_ref[1:2] = prepare(own_gram, gram_a_ref[...], vh_ref, vm_ref, vl_ref)
    right_ref[...] = scatter_finish(scatters, parts_ref) / scales
    for copy in copies[:-1] + forwards + scatters:
        copy.wait_send()


def third_exchange(n, raw_ref, all_out_ref, all_ref, gather_sems, forward_sems):
    place = Place(n)
    wait_barrier = place.greet()
    wait_barrier()
    gathers = gather_start(place, raw_ref, all_ref, gather_sems)
    gathers = gather_finish(place, gathers, all_ref, forward_sems)
    all_out_ref[...] = all_ref[...]
    for copy in gathers:
        copy.wait_send()


def f32(*shape):
    return jax.ShapeDtypeStruct(shape, jnp.float32)


def call(kernel, name, out_shape, scratch, collective_id=None, in_specs=None, limit=VMEM_LIMIT):
    vmem = pl.BlockSpec(memory_space=pltpu.VMEM)
    params = {} if collective_id is None else {"collective_id": collective_id, "has_side_effects": True}
    return pl.pallas_call(
        kernel,
        name=name,
        out_shape=out_shape,
        **({} if in_specs is None else {"in_specs": in_specs}),
        out_specs=jax.tree.map(lambda _: vmem, out_shape),
        scratch_shapes=scratch,
        compiler_params=pltpu.CompilerParams(vmem_limit_bytes=limit, **params),
    )


def on_device(tensor, init_second, init_third):
    local_rows, second_cells, depth_cells = tensor.shape
    rank = init_second.shape[1]
    n = lax.axis_size("row")
    chips = n // 2
    total_first = local_rows * n
    second_own, depth_own = second_cells // n, depth_cells // n
    system = [jax.ShapeDtypeStruct((rank, rank), jnp.bfloat16)] * 3
    split = [pltpu.VMEM((rank, rank), jnp.bfloat16)] * 3
    gather_sems = pltpu.SemaphoreType.DMA((2, chips))

    def buffers(rows, share):
        return [
            pltpu.VMEM((n, rows, rank), jnp.float32),
            pltpu.VMEM((2, chips, share, rank), jnp.float32),
            pltpu.VMEM((chips, share, rank), jnp.float32),
            pltpu.VMEM((chips, share, rank), jnp.float32),
            gather_sems,
            gather_sems,
            gather_sems,
        ]

    def solve(right, scales, parts, factor):
        rows = right.shape[0]
        padded = -(-rows // 8) * 8
        if padded != rows:
            right = jnp.pad(right, ((0, padded - rows), (0, 0)))
        raw, out = call(solve_kernel, "solve", (f32(padded, rank), f32(*factor.shape)), [])(
            right, scales, *parts, factor
        )
        return raw[:rows], out

    staged = [pltpu.VMEM(whole.shape, jnp.float32) for whole in (tensor, init_second, init_third)]
    raw_a = call(
        first_kernel,
        "first",
        f32(local_rows, rank),
        split + staged + [pltpu.SemaphoreType.DMA((3,))],
        in_specs=[pl.BlockSpec(memory_space=pltpu.HBM)] * 3,
        limit=FIRST_LIMIT,
    )(tensor, init_second, init_third)
    factor_first, gram_a, right_b, scales_b, *parts_b = call(
        functools.partial(first_exchange, n),
        "first_exchange",
        (f32(local_rows, rank), f32(rank, rank), f32(second_own, rank), f32(2, rank), *system),
        buffers(local_rows, second_own),
        0,
    )(raw_a, tensor, init_third)
    raw_b, factor_first_out = solve(right_b, scales_b, parts_b, factor_first)
    factor_second, right_c, scales_c, *parts_c = call(
        functools.partial(second_exchange, n),
        "second_exchange",
        (f32(second_own, rank), f32(depth_own, rank), f32(2, rank), *system),
        buffers(second_own, depth_own)
        + [pltpu.VMEM((chips, depth_cells, local_rows * second_cells // chips), jnp.float32)],
        1,
    )(raw_b, tensor, factor_first, gram_a)
    raw_c, factor_second_out = solve(right_c, scales_c, parts_c, factor_second)
    all_c = call(
        functools.partial(third_exchange, n),
        "third_exchange",
        f32(n, depth_own, rank),
        [pltpu.VMEM((n, depth_own, rank), jnp.float32), gather_sems, gather_sems],
        2,
    )(raw_c)
    factor_third, weights = call(
        functools.partial(last_kernel, total_first * second_cells),
        "last",
        (f32(n, depth_own, rank), f32(1, rank)),
        [],
    )(all_c)
    return (
        factor_first_out,
        factor_second_out,
        factor_third.reshape(depth_cells, rank),
        weights.reshape(rank),
    )


def solution(mesh):
    in_specs = (P(("groups", "row"), None, None), P("groups", None), P("groups", None))
    out_specs = (
        P(("groups", "row"), None),
        P(("groups", "row"), None),
        P("groups", None),
        P("groups"),
    )
    return jax.shard_map(
        on_device, mesh=mesh, in_specs=in_specs, out_specs=out_specs, check_vma=False
    )
```
